32 devices in a mesh: dom: 4 (over y, core), shard: 4 (over z), dp: 2 (over x).
Axes of the slice: x: 2, y: 2, z: 4, core: 2. Of those that a mesh axis runs over, the one named last changes fastest.
Arguments:
- queries_in: bfloat16 [4, 1024, 1024], P('dom', ('shard', 'dp')), may hold values from -8 to 8
- encoder_weight: bfloat16 [1024, 1024], P(('dom', 'shard', 'dp')), may hold values from -0.1875 to 0.1875
- codebook: float32 [4, 128, 8, 256], P('dom', 'shard'), may hold values from -0.06 to 0.06
- codes: int32 [4, 4096, 128], P('dom', 'shard'), may hold values from 0 to 255
- positive_ids: int32 [4, 1024], P('dom'), may hold values from 0 to 4095
- loss_weight: bfloat16 [4, 1024], P('dom'), may hold values from 0.5 to 2
Outputs:
- encoder_grad: float32 [1024, 1024], P(('dom', 'shard', 'dp'))
- codebook_grad: float32 [4, 128, 8, 256], P('dom', ('shard', 'dp'))
The draws below stay inside these ranges and needn't reach their ends.
All inputs are finite; a program needn't handle non-finite values.
Results may differ from the reference program's by a relative error of at most 0.0005.
The reference program's roundings to bfloat16 on the way (of `normed_low`, `book`, `passages`, `grad_scores` and `grad_encoded`) count: a program that leaves them out, or rounds other values in their place, can miss the bound.
Values may be sent and summed in bfloat16 or wider, within the bound.
No kernel may reach another device: no remote copies, remote signals or barrier semaphores. Data moves between devices by JAX's collectives and lax.ppermute only.
A program may use at most 64 MiB of HBM per device.

```python
import math
import jax
import jax.numpy as jnp
from jax import lax

D = 1024
M = 128
K = 256
SUB = 8
PARTS_SIZE = 4
QUERIES = 1024
PASSAGES = 4096


def draw_queries_in(key, part):
    keys = jax.random.split(key, 4)
    base = jax.random.normal(keys[0], (PARTS_SIZE, QUERIES, D), jnp.float32)
    rows = jnp.exp(jax.random.uniform(keys[1], (PARTS_SIZE, QUERIES, 1), jnp.float32, math.log(0.3), math.log(3.0)))
    cols = jnp.exp(jax.random.uniform(keys[3], (D,), jnp.float32, math.log(0.5), math.log(2.0)))
    values = base * rows * cols
    return jnp.clip(values, -8.0, 8.0).astype(jnp.bfloat16)


def place_ends(result, key, low, largest):
    shape = result.shape
    place = [jax.random.randint(jax.random.fold_in(key, axis), (), 0, shape[axis]) for axis in range(len(shape))]
    result = result.at[tuple(place)].set(low)
    longest = shape.index(max(shape))
    place[longest] = (place[longest] + 1) % shape[longest]
    return result.at[tuple(place)].set(largest)


def block_levels(own_key, shape, cuts, smallest, largest):
    gain, own = 1.0, jax.random.fold_in(own_key, 6)
    for position, shards_of in cuts:
        heights = jnp.exp(jax.random.uniform(jax.random.fold_in(own, position), (shards_of,), jnp.float32, smallest / len(cuts), largest / len(cuts)))
        gain = gain * jnp.repeat(heights, shape[position] // shards_of).reshape([-1 if axis == position else 1 for axis in range(len(shape))])
    return gain


def bell_draw(key, dims, deviation, bound, shards=(), held_as=jnp.bfloat16):
    drawn = jax.random.normal(key, dims, jnp.float32) * deviation
    if len(shards) > 0:
        drawn = block_levels(key, dims, shards, -0.22, 0.18) * drawn
    return jnp.clip(drawn, min=-bound, max=bound).astype(held_as)


def setup_inputs(seed: int = 0) -> dict:
    streams_of = jax.random.split(jax.random.key(seed), 7)
    queries_in = draw_queries_in(jax.random.fold_in(streams_of[6], 71), 0)
    encoder_weight = bell_draw(streams_of[1], (D, D), D ** -0.5, 0.1875, ((0, 32),))
    codebook = jnp.clip(jax.random.uniform(streams_of[2], (PARTS_SIZE, M, SUB, K), jnp.float32, -0.06, 0.06) * block_levels(streams_of[2], (PARTS_SIZE, M, SUB, K), ((0, 4), (1, 4)), -0.4, 0.0), -0.06, 0.06)
    codes = place_ends(jax.random.randint(streams_of[3], (PARTS_SIZE, PASSAGES, M), 0, K), jax.random.fold_in(streams_of[3], 1), 0, K - 1).astype(jnp.int32)
    positive_ids = place_ends(jax.random.randint(streams_of[4], (PARTS_SIZE, QUERIES), 0, PASSAGES), jax.random.fold_in(streams_of[4], 1), 0, PASSAGES - 1).astype(jnp.int32)
    loss_weight = jnp.clip(jnp.exp(math.log(2.0) - 1.3862944 * jax.random.uniform(streams_of[5], (PARTS_SIZE, QUERIES), jnp.float32) ** block_levels(streams_of[5], (PARTS_SIZE, QUERIES), ((0, 4),), -0.2, 0.2)), 0.5, 2.0).astype(jnp.bfloat16)
    return dict(queries_in=queries_in, encoder_weight=encoder_weight, codebook=codebook, codes=codes, positive_ids=positive_ids, loss_weight=loss_weight)


def rebuild(codes_part, book):
    levels = jnp.arange(K, dtype=jnp.int32)

    def one_sub(pair):
        column, words = pair
        onehot = (column[:, None] == levels[None, :]).astype(jnp.bfloat16)
        return lax.dot_general(onehot, words, (((1,), (1,)), ((), ())), preferred_element_type=jnp.float32)
    pieces = lax.map(one_sub, (codes_part.T, book))
    return jnp.transpose(pieces, (1, 0, 2)).reshape(codes_part.shape[0], -1).astype(jnp.bfloat16)

def word_grads(codes_part, grad_passages):
    levels = jnp.arange(K, dtype=jnp.int32)
    split = jnp.transpose(grad_passages.reshape(codes_part.shape[0], M, SUB), (1, 0, 2))

    def one_sub(pair):
        column, grads = pair
        onehot = (column[:, None] == levels[None, :]).astype(jnp.float32)
        return lax.dot_general(grads, onehot, (((0,), (0,)), ((), ())), precision=lax.Precision.HIGHEST, preferred_element_type=jnp.float32)
    return lax.map(one_sub, (codes_part.T, split))

def reference(queries_in, encoder_weight, codebook, codes, positive_ids, loss_weight):

    def partition(items):
        inputs, master, codes_part, positive, weights = items
        encoded = jnp.dot(inputs, encoder_weight, preferred_element_type=jnp.float32)
        inv_rms = lax.rsqrt(lax.optimization_barrier(jnp.mean(encoded * encoded, axis=1, keepdims=True)) + 1e-06)
        normed = encoded * inv_rms
        normed_low = normed.astype(jnp.bfloat16)
        passages = rebuild(codes_part, master.astype(jnp.bfloat16))
        scores = lax.dot_general(normed_low, passages, (((1,), (1,)), ((), ())), preferred_element_type=jnp.float32)
        exps = jnp.exp(scores)
        prob = exps / lax.optimization_barrier(jnp.sum(exps, axis=1, keepdims=True))
        target = (positive[:, None] == jnp.arange(PASSAGES, dtype=jnp.int32)[None, :]).astype(jnp.float32)
        grad_scores = (weights.astype(jnp.float32)[:, None] * (prob - target)).astype(jnp.bfloat16)
        grad_normed = jnp.dot(grad_scores, passages, preferred_element_type=jnp.float32)
        grad_passages = lax.dot_general(grad_scores, normed_low, (((0,), (0,)), ((), ())), preferred_element_type=jnp.float32)
        book_grad = word_grads(codes_part, grad_passages)
        inner = lax.optimization_barrier(jnp.mean(grad_normed * normed, axis=1, keepdims=True))
        grad_encoded = (inv_rms * (grad_normed - normed * inner)).astype(jnp.bfloat16)
        weight_grad = lax.dot_general(inputs, grad_encoded, (((0,), (0,)), ((), ())), preferred_element_type=jnp.float32)
        return (weight_grad, book_grad)
    weight_grads, book_grads = lax.map(partition, (queries_in, codebook, codes, positive_ids, loss_weight))
    return (lax.optimization_barrier(jnp.sum(weight_grads, axis=0)), book_grads)
```

```python
import functools
import jax
import jax.numpy as jnp
from jax import lax
from jax.experimental import pallas as pl
from jax.experimental.pallas import tpu as pltpu
from jax.sharding import PartitionSpec as P


BF16, F32, I32 = jnp.bfloat16, jnp.float32, jnp.int32
NT = (((1,), (1,)), ((), ()))
LANES = 128
SPLIT = 4
ANY = pl.BlockSpec(memory_space=pl.ANY)
VMEM = pl.BlockSpec(memory_space=pltpu.VMEM)
SMEM = pl.BlockSpec(memory_space=pltpu.SMEM)
LIMIT = 60 * 2**20


def ring(n, k):
    return [(i, (i + k) % n) for i in range(n)]


def flip(n, k):
    return [(i, i ^ k) for i in range(n)]


def cost(flops, bytes_accessed):
    return pl.CostEstimate(flops=flops, bytes_accessed=bytes_accessed, transcendentals=0)


def rebuild_kernel(place_ref, code_ref, *refs):
    books, (out_ref, codes_ref) = refs[:-2], refs[-2:]
    columns = code_ref.shape[1]
    codes_ref[...] = code_ref[...].astype(I32)
    for piece, book_ref in enumerate(books):
        held, sub, words = book_ref.shape
        first = place_ref[piece] * held

        def body(j, _, book_ref=book_ref, first=first):
            rows = pl.multiple_of(first + 8 * j, 8)
            codes = codes_ref[pl.ds(rows, 8), :]
            for pair in range(4):
                tables = []
                for h in range(2):
                    words_of = book_ref[8 * j + 2 * pair + h].astype(F32)
                    tables.append([words_of[:, c : c + LANES] for c in range(0, words, LANES)])
                for t in range(0, columns, LANES):
                    parts = []
                    for h in range(2):
                        row = codes[2 * pair + h : 2 * pair + h + 1, t : t + LANES]
                        index = jnp.broadcast_to(row, (sub, LANES))
                        lane = index & (LANES - 1)
                        value = None
                        for c, table in enumerate(tables[h]):
                            found = jnp.take_along_axis(table, lane, axis=1, mode="promise_in_bounds")
                            value = found if value is None else jnp.where(index < c * LANES, value, found)
                        parts.append(value)
                    out_rows = pl.ds(pl.multiple_of((rows + 2 * pair) * sub, 2 * sub), 2 * sub)
                    out_ref[out_rows, t : t + LANES] = jnp.concatenate(parts, 0).astype(BF16)
            return 0

        lax.fori_loop(0, held // 8, body, 0)


def rebuild(place, codes, books):
    subspaces, columns = codes.shape
    sub = books[0].shape[1]
    return pl.pallas_call(
        rebuild_kernel,
        out_shape=(
            jax.ShapeDtypeStruct((subspaces * sub, columns), BF16),
            jax.ShapeDtypeStruct((subspaces, columns), I32),
        ),
        in_specs=[SMEM, VMEM] + [VMEM] * len(books),
        out_specs=(VMEM, VMEM),
        compiler_params=pltpu.CompilerParams(vmem_limit_bytes=16 * 2**20),
        cost_estimate=cost(2 * 10**9, 4 * 10**6),
    )(place, codes, *books)


def main_kernel(n_q, n_w, n_t, woff_ref, tbase_ref, frow_ref, pos_ref, wt_ref, *refs):
    q_refs, refs = refs[:n_q], refs[n_q:]
    w_refs, refs = refs[:n_w], refs[n_w:]
    t_refs, refs = refs[:n_t], refs[n_t:]
    gs_ref, nt_ref, own_ref, other_ref = refs[:4]
    w, q, tiles, exps, normed, total, gn, wsem, tsem = refs[4:]
    copies = []
    for i, w_ref in enumerate(w_refs):
        blocks, rows = w_ref.shape[0], w_ref.shape[1]
        for k in range(blocks):
            n = i * blocks + k
            to = w.at[pl.ds(pl.multiple_of(woff_ref[n], rows), rows), :]
            copies.append(pltpu.make_async_copy(w_ref.at[k], to, wsem.at[n]))
    for copy in copies:
        copy.start()
    for j, t_ref in enumerate(t_refs):
        pltpu.make_async_copy(t_ref, tiles.at[j], tsem.at[j]).start()
    own = q_refs[0].shape[0]
    for i, q_ref in enumerate(q_refs):
        q[i * own : (i + 1) * own, :] = q_ref[...]
    depth = q.shape[1]
    rows = frow_ref.shape[0]
    pick = (frow_ref[...] == lax.broadcasted_iota(I32, (rows, depth), 1)).astype(F32).astype(BF16)
    picked = lax.dot_general(pick, q[...], NT, preferred_element_type=F32).astype(BF16)
    for copy in copies:
        copy.wait()
    encoded = jnp.dot(q[...], w[...], preferred_element_type=F32)
    inv_rms = lax.rsqrt(jnp.mean(encoded * encoded, axis=1, keepdims=True) + 1e-06)
    normed[...] = encoded * inv_rms
    low = normed[...].astype(BF16)
    q[...] = low
    nt_ref[...] = low.T
    total[...] = jnp.zeros_like(total)
    width = tiles.shape[2]

    def score(j, _):
        pltpu.make_async_copy(t_refs[0], tiles.at[j], tsem.at[j]).wait()
        e = jnp.exp(jnp.dot(q[...], tiles[j], preferred_element_type=F32))
        exps[j] = e
        total[...] += jnp.sum(e, axis=1, keepdims=True)
        return 0

    lax.fori_loop(0, n_t, score, 0)
    gn[...] = jnp.zeros_like(gn)
    scale = 1.0 / total[...]

    def back(j, _):
        ids = tbase_ref[j] + lax.broadcasted_iota(I32, (1, width), 1)
        target = (pos_ref[...] == ids).astype(F32)
        gs = (wt_ref[...] * (exps[j] * scale - target)).astype(BF16)
        gs_ref[j] = gs
        gn[...] += lax.dot_general(gs, tiles[j], NT, preferred_element_type=F32)
        return 0

    lax.fori_loop(0, n_t, back, 0)
    inner = jnp.mean(gn[...] * normed[...], axis=1, keepdims=True)
    grad = (inv_rms * (gn[...] - normed[...] * inner)).astype(BF16)
    half = rows // 2
    own_ref[...] = jnp.dot(picked[:half], grad, preferred_element_type=F32)
    other_ref[...] = jnp.dot(picked[half:], grad, preferred_element_type=F32)


def main(woff, tbase, frow, pos, wt, q_pieces, w_pieces, t_pieces):
    n_q, n_w, n_t = len(q_pieces), len(w_pieces), len(t_pieces)
    own, depth = q_pieces[0].shape
    queries = own * n_q
    features, width = t_pieces[0].shape
    half = frow.shape[0] // 2
    return pl.pallas_call(
        functools.partial(main_kernel, n_q, n_w, n_t),
        out_shape=(
            jax.ShapeDtypeStruct((n_t, queries, width), BF16),
            jax.ShapeDtypeStruct((features, queries), BF16),
            jax.ShapeDtypeStruct((half, features), F32),
            jax.ShapeDtypeStruct((half, features), F32),
        ),
        in_specs=[SMEM, SMEM, VMEM, VMEM, VMEM] + [VMEM] * n_q + [ANY] * (n_w + n_t),
        out_specs=(VMEM,) * 4,
        scratch_shapes=[
            pltpu.VMEM((depth, features), BF16),
            pltpu.VMEM((queries, depth), BF16),
            pltpu.VMEM((n_t, features, width), BF16),
            pltpu.VMEM((n_t, queries, width), F32),
            pltpu.VMEM((queries, features), F32),
            pltpu.VMEM((queries, 1), F32),
            pltpu.VMEM((queries, features), F32),
            pltpu.SemaphoreType.DMA((woff.shape[0],)),
            pltpu.SemaphoreType.DMA((n_t,)),
        ],
        compiler_params=pltpu.CompilerParams(vmem_limit_bytes=LIMIT),
        cost_estimate=cost(20 * 10**9, 20 * 10**6),
    )(woff, tbase, frow, pos, wt, *q_pieces, *w_pieces, *t_pieces)


def words_kernel(n_t, words, block_ref, nt_ref, gs_ref, *refs):
    code_refs, (out_ref, grads, codes) = refs[:n_t], refs[n_t:]
    j = pl.program_id(0)
    width = gs_ref.shape[2]
    span = pl.ds(pl.multiple_of(j * width, width), width)
    grads[:, span] = jnp.dot(nt_ref[...], gs_ref[0], preferred_element_type=F32)

    @pl.when(j == n_t - 1)
    def _():
        for i, code_ref in enumerate(code_refs):
            codes[:, i * width : (i + 1) * width] = code_ref[...]
        held, sub = out_ref.shape[0], out_ref.shape[1]
        low = words // SPLIT
        shift = low.bit_length() - 1
        step = 1024

        def body(group, _):
            code8 = codes[pl.ds(pl.multiple_of(8 * group, 8), 8), :]
            for i in range(8):
                m = 8 * group + i
                grad = grads[pl.ds(pl.multiple_of(sub * m, sub), sub), :]
                upper = grad.astype(BF16).astype(F32)
                parts = jnp.concatenate([upper, grad - upper], 0)
                row = code8[i : i + 1, :]
                acc = None
                for t in range(0, codes.shape[1], step):
                    c = row[:, t : t + step]
                    p = parts[:, t : t + step]
                    high = jnp.broadcast_to(lax.shift_right_logical(c, shift), p.shape)
                    p = jnp.concatenate([jnp.where(high == h, p, 0.0) for h in range(SPLIT)], 0)
                    hot = (c & (low - 1)) == lax.broadcasted_iota(I32, (low, step), 0)
                    r = lax.dot_general(
                        hot.astype(F32).astype(BF16), p.astype(BF16), NT, preferred_element_type=F32
                    )
                    acc = r if acc is None else acc + r
                acc = acc.T
                pieces = []
                for h in range(SPLIT):
                    a = acc[2 * sub * h : 2 * sub * h + sub]
                    pieces.append(a + acc[2 * sub * h + sub : 2 * sub * (h + 1)])
                out_ref[m] = jnp.concatenate(pieces, 1)
            return 0

        lax.fori_loop(0, held // 8, body, 0)


def word_grads(block, held, words, nt, gs, codes):
    n_t, queries, width = gs.shape
    sub = nt.shape[0] // codes[0].shape[0]
    return pl.pallas_call(
        functools.partial(words_kernel, n_t, words),
        out_shape=jax.ShapeDtypeStruct((held, sub, words), F32),
        grid_spec=pltpu.PrefetchScalarGridSpec(
            num_scalar_prefetch=1,
            grid=(n_t,),
            in_specs=[
                pl.BlockSpec((held * sub, queries), lambda j, b: (b[0], 0)),
                pl.BlockSpec((1, queries, width), lambda j, b: (j, 0, 0)),
            ]
            + [pl.BlockSpec((held, width), lambda j, b: (b[0], 0))] * n_t,
            out_specs=pl.BlockSpec((held, sub, words), lambda j, b: (0, 0, 0)),
            scratch_shapes=[
                pltpu.VMEM((held * sub, n_t * width), F32),
                pltpu.VMEM((held, n_t * width), I32),
            ],
        ),
        compiler_params=pltpu.CompilerParams(vmem_limit_bytes=LIMIT),
        cost_estimate=cost(6 * 10**9, 6 * 10**6),
    )(block, nt, gs, *codes)


def per_device(n_dom, n_sh, n_dp, queries_in, encoder_weight, codebook, codes, positive_ids, loss_weight):
    dom, z, x = (lax.axis_index(a) for a in ("dom", "shard", "dp"))
    n_dev = n_dom * n_sh * n_dp
    n_zp = n_sh // 2
    evens = range(0, n_dom, 2)
    shards = [lax.rem(z - k + n_sh, n_sh) for k in range(n_sh)]
    lanes = [lax.rem(x - t + n_dp, n_dp) for t in range(n_dp)]
    move = lax.ppermute

    w_rows, depth = encoder_weight.shape
    w_z = jnp.stack([encoder_weight] + [move(encoder_weight, "shard", ring(n_sh, k)) for k in range(1, n_sh)])

    q = queries_in[0]
    own = q.shape[0]
    q_pieces, q_from = [], []
    for t in range(n_dp):
        for a in range(2):
            pairs = []
            for s in range(n_sh):
                for d in range(n_dp):
                    pairs.append((s * n_dp + d, (s ^ a) * n_dp + (d + t) % n_dp))
            q_pieces.append(q if t == a == 0 else move(q, ("shard", "dp"), pairs))
            q_from.append((z ^ a) * n_dp + lanes[t])

    book = codebook[0].astype(BF16)
    words = book.shape[2]
    books = [book] + [move(book, "shard", ring(n_sh, k)) for k in range(1, n_sh)]
    codes_t = codes[0].T.astype(BF16)
    subspaces, pass_rows = codes_t.shape
    width = pass_rows // n_dp
    share = [lax.dynamic_slice_in_dim(codes_t, lanes[t] * width, width, 1) for t in range(n_dp)]
    tiles = {(0, 0): share[0]}
    for k in range(1, n_sh):
        tiles[0, k] = move(share[0], "shard", ring(n_sh, k))
    for t in range(1, n_dp):
        tiles[t, 0] = share[t]
        for k in range(1, n_sh):
            tiles[t, k] = move(tiles[0, k], "dp", ring(n_dp, t))

    w_x = [w_z] + [move(w_z, "dp", ring(n_dp, t)) for t in range(1, n_dp)]
    w_pieces, w_places = [], []
    for e in evens:
        for t in range(n_dp):
            w_pieces.append(w_x[t] if e == 0 else move(w_x[t], "dom", flip(n_dom, e)))
    w_pieces += [move(piece, "dom", flip(n_dom, 1)) for piece in w_pieces]
    for core in range(2):
        for e in evens:
            for t in range(n_dp):
                for k in range(n_sh):
                    w_places.append(((dom ^ (e | core)) * n_sh + shards[k]) * n_dp + lanes[t])
    w_places = jnp.stack(w_places).astype(I32)
    if w_rows % 16:
        whole = jnp.concatenate(w_pieces).reshape(n_dev, w_rows, depth)
        order = jnp.zeros((n_dev,), I32).at[w_places].set(jnp.arange(n_dev, dtype=I32))
        w_pieces = [whole[order].reshape(1, n_dev * w_rows, depth)]
        w_offsets = jnp.zeros((1,), I32)
    else:
        w_offsets = w_places * w_rows

    place = jnp.stack(shards).astype(I32)
    order = sorted(tiles)
    bases = [shards[k] * pass_rows + lanes[t] * width for t, k in order]
    built = [rebuild(place, tiles[key], books) for key in order]
    passages = [b[0] for b in built]
    tile_codes = [b[1] for b in built]

    def rows_of(array):
        return jnp.concatenate([lax.dynamic_slice_in_dim(array, f * own, own, 0) for f in q_from])[:, None]

    out_rows = depth // n_dev
    zp, zi = z // 2, z % 2
    blocks = []
    for core in range(2):
        for e in evens:
            for j in range(n_zp):
                to_z = lax.rem(zp + j, n_zp) * 2 + zi
                blocks.append((((dom ^ (e | core)) * n_sh + to_z) * n_dp + x) * out_rows)
    frow = (jnp.stack(blocks).astype(I32)[:, None] + jnp.arange(out_rows, dtype=I32)[None, :]).reshape(-1, 1)

    gs, low_t, own_part, other_part = main(
        w_offsets,
        jnp.stack(bases).astype(I32),
        frow,
        rows_of(positive_ids[0]),
        rows_of(loss_weight[0].astype(F32)),
        q_pieces,
        w_pieces,
        passages,
    )

    own_part = (own_part + move(other_part, "dom", flip(n_dom, 1))).reshape(len(evens), n_zp, out_rows, depth)
    weight_grad = own_part[0, 0]
    for i, e in enumerate(evens):
        for j in range(n_zp):
            if i == j == 0:
                continue
            pairs = []
            for d in range(n_dom):
                for s in range(n_sh):
                    pairs.append((d * n_sh + s, (d ^ e) * n_sh + (s + 2 * j) % n_sh))
            weight_grad = weight_grad + move(own_part[i, j], ("dom", "shard"), pairs)

    held = subspaces // (n_sh * n_dp)
    book_grad = None
    for j in reversed(range(n_zp)):
        to_z = lax.rem(zp + j, n_zp) * 2 + zi
        block = (to_z * n_dp + x).astype(I32)[None]
        part = word_grads(block, held, words, low_t, gs, tile_codes)
        if j:
            part = move(part, "shard", ring(n_sh, 2 * j))
        book_grad = part if book_grad is None else book_grad + part
    return (weight_grad, book_grad[None])


def solution(mesh):
    sizes = [mesh.shape[a] for a in ("dom", "shard", "dp")]
    return jax.shard_map(
        functools.partial(per_device, *sizes),
        mesh=mesh,
        in_specs=(
            P("dom", ("shard", "dp"), None),
            P(("dom", "shard", "dp"), None),
            P("dom", "shard", None, None),
            P("dom", "shard", None),
            P("dom", None),
            P("dom", None),
        ),
        out_specs=(P(("dom", "shard", "dp"), None), P("dom", ("shard", "dp"), None, None)),
        check_vma=False,
    )
```

```python
import functools
import jax
import jax.numpy as jnp
from jax import lax
from jax.experimental import pallas as pl
from jax.experimental.pallas import tpu as pltpu
from jax.sharding import PartitionSpec as P


BF16, F32, I32 = jnp.bfloat16, jnp.float32, jnp.int32
NT = (((1,), (1,)), ((), ()))
LANES = 128
SPLIT = 4
ANY = pl.BlockSpec(memory_space=pl.ANY)
VMEM = pl.BlockSpec(memory_space=pltpu.VMEM)
SMEM = pl.BlockSpec(memory_space=pltpu.SMEM)
MIB = 2**20


def ring(n, k):
    return [(i, (i + k) % n) for i in range(n)]


def flip(n, k):
    return [(i, i ^ k) for i in range(n)]


def cost(flops, bytes_accessed):
    return pl.CostEstimate(flops=flops, bytes_accessed=bytes_accessed, transcendentals=0)


def rebuild_kernel(n_t, n_b, place_ref, *refs):
    code_refs, books, (out_ref, codes_ref, table) = refs[:n_t], refs[n_t : n_t + n_b], refs[n_t + n_b :]
    held, sub, words = books[0].shape
    columns = code_refs[0].shape[1]
    for i, code_ref in enumerate(code_refs):
        codes_ref[i] = code_ref[...].astype(I32)
    for piece, book_ref in enumerate(books):
        table[pl.ds(place_ref[piece] * held, held)] = book_ref[...].astype(F32)

    def body(i, _):
        tile, first = i // n_b, lax.rem(i, n_b) * held
        for j in range(held // 8):
            rows = pl.multiple_of(first + 8 * j, 8)
            codes = codes_ref[tile, pl.ds(rows, 8), :]
            for pair in range(4):
                tables = []
                for h in range(2):
                    words_of = table[rows + 2 * pair + h]
                    tables.append([words_of[:, c : c + LANES] for c in range(0, words, LANES)])
                for t in range(0, columns, LANES):
                    parts = []
                    for h in range(2):
                        row = codes[2 * pair + h : 2 * pair + h + 1, t : t + LANES]
                        index = jnp.broadcast_to(row, (sub, LANES))
                        lane = index & (LANES - 1)
                        value = None
                        for c, part in enumerate(tables[h]):
                            found = jnp.take_along_axis(part, lane, axis=1, mode="promise_in_bounds")
                            value = found if value is None else jnp.where(index < c * LANES, value, found)
                        parts.append(value)
                    out_rows = pl.ds(pl.multiple_of((rows + 2 * pair) * sub, 2 * sub), 2 * sub)
                    out_ref[tile, out_rows, t : t + LANES] = jnp.concatenate(parts, 0).astype(BF16)
        return 0

    lax.fori_loop(0, n_t * n_b, body, 0)


def rebuild(place, codes, books):
    n_t, n_b = len(codes), len(books)
    subspaces, columns = codes[0].shape
    _, sub, words = books[0].shape
    return pl.pallas_call(
        functools.partial(rebuild_kernel, n_t, n_b),
        out_shape=(
            jax.ShapeDtypeStruct((n_t, subspaces * sub, columns), BF16),
            jax.ShapeDtypeStruct((n_t, subspaces, columns), I32),
        ),
        in_specs=[SMEM] + [VMEM] * (n_t + n_b),
        out_specs=(VMEM, VMEM),
        scratch_shapes=[pltpu.VMEM((subspaces, sub, words), F32)],
        compiler_params=pltpu.CompilerParams(vmem_limit_bytes=(6 + n_t) * MIB),
        cost_estimate=cost(n_t * 10**9, n_t * 2 * 10**6),
    )(place, *codes, *books)


def main_kernel(n_q, n_w, n_g, woff_ref, tbase_ref, frow_ref, pos_ref, wt_ref, *refs):
    q_refs, refs = refs[:n_q], refs[n_q:]
    w_refs, refs = refs[:n_w], refs[n_w:]
    g_refs, refs = refs[:n_g], refs[n_g:]
    gs_ref, nt_ref, own_ref, other_ref = refs[:4]
    w, q, exps, normed, total, gn = refs[4:]
    for i, w_ref in enumerate(w_refs):
        blocks, rows = w_ref.shape[0], w_ref.shape[1]
        for k in range(blocks):
            w[pl.ds(pl.multiple_of(woff_ref[i * blocks + k], rows), rows), :] = w_ref[k]
    own = q_refs[0].shape[0]
    for i, q_ref in enumerate(q_refs):
        q[i * own : (i + 1) * own, :] = q_ref[...]
    depth = q.shape[1]
    rows = frow_ref.shape[0]
    pick = (frow_ref[...] == lax.broadcasted_iota(I32, (rows, depth), 1)).astype(F32).astype(BF16)
    picked = lax.dot_general(pick, q[...], NT, preferred_element_type=F32).astype(BF16)
    encoded = jnp.dot(q[...], w[...], preferred_element_type=F32)
    inv_rms = lax.rsqrt(jnp.mean(encoded * encoded, axis=1, keepdims=True) + 1e-06)
    normed[...] = encoded * inv_rms
    low = normed[...].astype(BF16)
    q[...] = low
    nt_ref[...] = low.T
    total[...] = jnp.zeros_like(total)
    first = 0
    for tiles in g_refs:

        def score(j, _, tiles=tiles, first=first):
            e = jnp.exp(jnp.dot(q[...], tiles[j], preferred_element_type=F32))
            exps[first + j] = e
            total[...] += jnp.sum(e, axis=1, keepdims=True)
            return 0

        lax.fori_loop(0, tiles.shape[0], score, 0)
        first += tiles.shape[0]
    gn[...] = jnp.zeros_like(gn)
    scale = 1.0 / total[...]
    first = 0
    for tiles in g_refs:
        width = tiles.shape[2]

        def back(j, _, tiles=tiles, first=first, width=width):
            ids = tbase_ref[first + j] + lax.broadcasted_iota(I32, (1, width), 1)
            target = (pos_ref[...] == ids).astype(F32)
            gs = (wt_ref[...] * (exps[first + j] * scale - target)).astype(BF16)
            gs_ref[first + j] = gs
            gn[...] += lax.dot_general(gs, tiles[j], NT, preferred_element_type=F32)
            return 0

        lax.fori_loop(0, tiles.shape[0], back, 0)
        first += tiles.shape[0]
    inner = jnp.mean(gn[...] * normed[...], axis=1, keepdims=True)
    grad = (inv_rms * (gn[...] - normed[...] * inner)).astype(BF16)
    half = rows // 2
    own_ref[...] = jnp.dot(picked[:half], grad, preferred_element_type=F32)
    other_ref[...] = jnp.dot(picked[half:], grad, preferred_element_type=F32)


def main(woff, tbase, frow, pos, wt, q_pieces, w_pieces, groups):
    n_q, n_w, n_g = len(q_pieces), len(w_pieces), len(groups)
    own, depth = q_pieces[0].shape
    queries = own * n_q
    n_t = sum(g.shape[0] for g in groups)
    features, width = groups[0].shape[1:]
    half = frow.shape[0] // 2
    return pl.pallas_call(
        functools.partial(main_kernel, n_q, n_w, n_g),
        out_shape=(
            jax.ShapeDtypeStruct((n_t, queries, width), BF16),
            jax.ShapeDtypeStruct((features, queries), BF16),
            jax.ShapeDtypeStruct((half, features), F32),
            jax.ShapeDtypeStruct((half, features), F32),
        ),
        in_specs=[SMEM, SMEM, VMEM, VMEM, VMEM] + [VMEM] * (n_q + n_w + n_g),
        out_specs=(VMEM,) * 4,
        scratch_shapes=[
            pltpu.VMEM((depth, features), BF16),
            pltpu.VMEM((queries, depth), BF16),
            pltpu.VMEM((n_t, queries, width), F32),
            pltpu.VMEM((queries, features), F32),
            pltpu.VMEM((queries, 1), F32),
            pltpu.VMEM((queries, features), F32),
        ],
        compiler_params=pltpu.CompilerParams(vmem_limit_bytes=(28 if n_t * queries * width * 4 <= 8 * MIB else 60) * MIB),
        cost_estimate=cost(20 * 10**9, 20 * 10**6),
    )(woff, tbase, frow, pos, wt, *q_pieces, *w_pieces, *groups)


def dots_kernel(blocks_ref, nt_ref, gs_ref, *out_refs):
    rows = out_refs[0].shape[0]
    n_t, width = gs_ref.shape[0], gs_ref.shape[2]
    picked = [nt_ref[pl.ds(pl.multiple_of(blocks_ref[i] * rows, rows), rows), :] for i in range(len(out_refs))]
    picked = jnp.concatenate(picked, 0)
    for j in range(n_t):
        grads = jnp.dot(picked, gs_ref[j], preferred_element_type=F32)
        for i, out_ref in enumerate(out_refs):
            out_ref[:, j * width : (j + 1) * width] = grads[i * rows : (i + 1) * rows]


def passage_grads(blocks, rows, nt, gs):
    n_t, _, width = gs.shape
    n = blocks.shape[0]
    return pl.pallas_call(
        dots_kernel,
        out_shape=(jax.ShapeDtypeStruct((rows, n_t * width), F32),) * n,
        in_specs=[SMEM, VMEM, VMEM],
        out_specs=(VMEM,) * n,
        compiler_params=pltpu.CompilerParams(vmem_limit_bytes=12 * MIB),
        cost_estimate=cost(3 * 10**9, 8 * 10**6),
    )(blocks, nt, gs)


def words_kernel(words, block_ref, grads_ref, *refs):
    code_refs, (out_ref, codes) = refs[:-2], refs[-2:]
    held, sub = out_ref.shape[0], out_ref.shape[1]
    column = 0
    for code_ref in code_refs:
        width = code_ref.shape[2]
        for j in range(code_ref.shape[0]):
            rows = pl.ds(pl.multiple_of(block_ref[0] * held, held), held)
            codes[:, column : column + width] = code_ref[j, rows, :]
            column += width
    low = words // SPLIT
    shift = low.bit_length() - 1
    step = 1024

    def body(group, _):
        code8 = codes[pl.ds(pl.multiple_of(8 * group, 8), 8), :]
        for i in range(8):
            m = 8 * group + i
            grad = grads_ref[pl.ds(pl.multiple_of(sub * m, sub), sub), :]
            upper = grad.astype(BF16).astype(F32)
            parts = jnp.concatenate([upper, grad - upper], 0)
            row = code8[i : i + 1, :]
            acc = None
            for t in range(0, codes.shape[1], step):
                c = row[:, t : t + step]
                p = parts[:, t : t + step]
                high = jnp.broadcast_to(lax.shift_right_logical(c, shift), p.shape)
                p = jnp.concatenate([jnp.where(high == h, p, 0.0) for h in range(SPLIT)], 0)
                hot = (c & (low - 1)) == lax.broadcasted_iota(I32, (low, step), 0)
                r = lax.dot_general(
                    hot.astype(F32).astype(BF16), p.astype(BF16), NT, preferred_element_type=F32
                )
                acc = r if acc is None else acc + r
            acc = acc.T
            pieces = []
            for h in range(SPLIT):
                a = acc[2 * sub * h : 2 * sub * h + sub]
                pieces.append(a + acc[2 * sub * h + sub : 2 * sub * (h + 1)])
            out_ref[m] = jnp.concatenate(pieces, 1)
        return 0

    lax.fori_loop(0, held // 8, body, 0)


def word_grads(block, held, words, grads, codes):
    columns = grads.shape[1]
    sub = grads.shape[0] // held
    return pl.pallas_call(
        functools.partial(words_kernel, words),
        out_shape=jax.ShapeDtypeStruct((held, sub, words), F32),
        in_specs=[SMEM, VMEM] + [VMEM] * len(codes),
        out_specs=VMEM,
        scratch_shapes=[pltpu.VMEM((held, columns), I32)],
        compiler_params=pltpu.CompilerParams(vmem_limit_bytes=8 * MIB),
        cost_estimate=cost(3 * 10**9, 4 * 10**6),
    )(block, grads, *codes)


def compute(n_dom, n_sh, n_dp, queries_in, encoder_weight, codebook, codes, positive_ids, loss_weight):
    dom, z, x = (lax.axis_index(a) for a in ("dom", "shard", "dp"))
    n_dev = n_dom * n_sh * n_dp
    n_zp = n_sh // 2
    evens = range(0, n_dom, 2)
    shards = [lax.rem(z - k + n_sh, n_sh) for k in range(n_sh)]
    lanes = [lax.rem(x - t + n_dp, n_dp) for t in range(n_dp)]
    move = lax.ppermute

    w_rows, depth = encoder_weight.shape
    w_z = jnp.stack([encoder_weight] + [move(encoder_weight, "shard", ring(n_sh, k)) for k in range(1, n_sh)])

    q = queries_in[0]
    own = q.shape[0]
    q_pieces, q_from = [], []
    for t in range(n_dp):
        for a in range(2):
            pairs = []
            for s in range(n_sh):
                for d in range(n_dp):
                    pairs.append((s * n_dp + d, (s ^ a) * n_dp + (d + t) % n_dp))
            q_pieces.append(q if t == a == 0 else move(q, ("shard", "dp"), pairs))
            q_from.append((z ^ a) * n_dp + lanes[t])

    book = codebook[0].astype(BF16)
    words = book.shape[2]
    books = [book] + [move(book, "shard", ring(n_sh, k)) for k in range(1, n_sh)]
    codes_t = codes[0].T.astype(BF16)
    subspaces, pass_rows = codes_t.shape
    width = pass_rows // n_dp
    share = [lax.dynamic_slice_in_dim(codes_t, lanes[t] * width, width, 1) for t in range(n_dp)]
    tiles = {(0, 0): share[0]}
    for k in range(1, n_sh):
        tiles[0, k] = move(share[0], "shard", ring(n_sh, k))
    for t in range(1, n_dp):
        tiles[t, 0] = share[t]
        for k in range(1, n_sh):
            tiles[t, k] = move(tiles[0, k], "dp", ring(n_dp, t))

    w_x = [w_z] + [move(w_z, "dp", ring(n_dp, t)) for t in range(1, n_dp)]
    w_pieces, w_places = [], []
    for e in evens:
        for t in range(n_dp):
            w_pieces.append(w_x[t] if e == 0 else move(w_x[t], "dom", flip(n_dom, e)))
    w_pieces += [move(piece, "dom", flip(n_dom, 1)) for piece in w_pieces]
    for core in range(2):
        for e in evens:
            for t in range(n_dp):
                for k in range(n_sh):
                    w_places.append(((dom ^ (e | core)) * n_sh + shards[k]) * n_dp + lanes[t])
    w_places = jnp.stack(w_places).astype(I32)
    if w_rows % 16:
        whole = jnp.concatenate(w_pieces).reshape(n_dev, w_rows, depth)
        order = jnp.zeros((n_dev,), I32).at[w_places].set(jnp.arange(n_dev, dtype=I32))
        w_pieces = [whole[order].reshape(1, n_dev * w_rows, depth)]
        w_offsets = jnp.zeros((1,), I32)
    else:
        w_offsets = w_places * w_rows

    place = jnp.stack(shards).astype(I32)
    order = [[(t, 0) for t in range(n_dp)]] + [[(t, k) for k in range(1, n_sh)] for t in range(n_dp)]
    bases = [shards[k] * pass_rows + lanes[t] * width for group in order for t, k in group]
    built = [rebuild(place, [tiles[key] for key in group], books) for group in order]
    passages = [b[0] for b in built]
    tile_codes = [b[1] for b in built]

    def rows_of(array):
        return jnp.concatenate([lax.dynamic_slice_in_dim(array, f * own, own, 0) for f in q_from])[:, None]

    out_rows = depth // n_dev
    zp, zi = z // 2, z % 2
    blocks = []
    for core in range(2):
        for e in evens:
            for j in range(n_zp):
                to_z = lax.rem(zp + j, n_zp) * 2 + zi
                blocks.append((((dom ^ (e | core)) * n_sh + to_z) * n_dp + x) * out_rows)
    frow = (jnp.stack(blocks).astype(I32)[:, None] + jnp.arange(out_rows, dtype=I32)[None, :]).reshape(-1, 1)

    gs, low_t, own_part, other_part = main(
        w_offsets,
        jnp.stack(bases).astype(I32),
        frow,
        rows_of(positive_ids[0]),
        rows_of(loss_weight[0].astype(F32)),
        q_pieces,
        w_pieces,
        passages,
    )

    held = subspaces // (n_sh * n_dp)
    owners = [lax.rem(zp + j, n_zp) * 2 + zi for j in range(n_zp)]
    blocks = jnp.stack([o * n_dp + x for o in owners]).astype(I32)
    grads = passage_grads(blocks, low_t.shape[0] // (n_sh * n_dp), low_t, gs)

    summed = own_part + move(other_part, "dom", flip(n_dom, 1))
    summed, grads = lax.optimization_barrier((summed, grads))
    summed = summed.reshape(len(evens), n_zp, out_rows, depth)
    weight_grad = summed[0, 0]
    for i, e in enumerate(evens):
        for j in range(n_zp):
            if i == j == 0:
                continue
            pairs = []
            for d in range(n_dom):
                for s in range(n_sh):
                    pairs.append((d * n_sh + s, (d ^ e) * n_sh + (s + 2 * j) % n_sh))
            moved = move(summed[i, j], ("dom", "shard"), pairs)
            weight_grad = weight_grad + moved

    book_grad = None
    for j in reversed(range(n_zp)):
        part = word_grads(blocks[j : j + 1], held, words, grads[j], tile_codes)
        if j:
            part = move(part, "shard", ring(n_sh, 2 * j))
        book_grad = part if book_grad is None else book_grad + part
    return (weight_grad, book_grad[None])


def solution(mesh):
    sizes = [mesh.shape[a] for a in ("dom", "shard", "dp")]
    return jax.shard_map(
        functools.partial(compute, *sizes),
        mesh=mesh,
        in_specs=(
            P("dom", ("shard", "dp"), None),
            P(("dom", "shard", "dp"), None),
            P("dom", "shard", None, None),
            P("dom", "shard", None),
            P("dom", None),
            P("dom", None),
        ),
        out_specs=(P(("dom", "shard", "dp"), None), P("dom", ("shard", "dp"), None, None)),
        check_vma=False,
    )
```

```python
import functools
import jax
import jax.numpy as jnp
from jax import lax
from jax.experimental import pallas as pl
from jax.experimental.pallas import tpu as pltpu
from jax.sharding import PartitionSpec as P


BF16, F32, I32 = jnp.bfloat16, jnp.float32, jnp.int32
NT = (((1,), (1,)), ((), ()))
LANES = 128
SPLIT = 4
ANY = pl.BlockSpec(memory_space=pl.ANY)
VMEM = pl.BlockSpec(memory_space=pltpu.VMEM)
SMEM = pl.BlockSpec(memory_space=pltpu.SMEM)
MIB = 2**20


def ring(n, k):
    return [(i, (i + k) % n) for i in range(n)]


def flip(n, k):
    return [(i, i ^ k) for i in range(n)]


def cost(flops, bytes_accessed):
    return pl.CostEstimate(flops=flops, bytes_accessed=bytes_accessed, transcendentals=0)


def rebuild_kernel(n_t, n_b, place_ref, blocks_ref, *refs):
    code_refs, books = refs[:n_t], refs[n_t : n_t + n_b]
    out_ref, kept_ref, codes_ref, table = refs[n_t + n_b :]
    held, sub, words = books[0].shape
    columns = code_refs[0].shape[1]
    kept = kept_ref.shape[2]
    for i, code_ref in enumerate(code_refs):
        codes_ref[i] = code_ref[...].astype(I32)
        for b in range(kept_ref.shape[1]):
            kept_ref[i, b] = codes_ref[i, pl.ds(pl.multiple_of(blocks_ref[b] * kept, kept), kept), :]
    for piece, book_ref in enumerate(books):
        table[pl.ds(place_ref[piece] * held, held)] = book_ref[...].astype(F32)

    def body(i, _):
        tile, first = i // n_b, lax.rem(i, n_b) * held
        for j in range(held // 8):
            rows = pl.multiple_of(first + 8 * j, 8)
            codes = codes_ref[tile, pl.ds(rows, 8), :]
            for pair in range(4):
                tables = []
                for h in range(2):
                    words_of = table[rows + 2 * pair + h]
                    tables.append([words_of[:, c : c + LANES] for c in range(0, words, LANES)])
                for t in range(0, columns, LANES):
                    parts = []
                    for h in range(2):
                        row = codes[2 * pair + h : 2 * pair + h + 1, t : t + LANES]
                        index = jnp.broadcast_to(row, (sub, LANES))
                        lane = index & (LANES - 1)
                        value = None
                        for c, part in enumerate(tables[h]):
                            found = jnp.take_along_axis(part, lane, axis=1, mode="promise_in_bounds")
                            value = found if value is None else jnp.where(index < c * LANES, value, found)
                        parts.append(value)
                    out_rows = pl.ds(pl.multiple_of((rows + 2 * pair) * sub, 2 * sub), 2 * sub)
                    out_ref[tile, out_rows, t : t + LANES] = jnp.concatenate(parts, 0).astype(BF16)
        return 0

    lax.fori_loop(0, n_t * n_b, body, 0)


def rebuild(place, blocks, kept, codes, books):
    n_t, n_b = len(codes), len(books)
    subspaces, columns = codes[0].shape
    _, sub, words = books[0].shape
    return pl.pallas_call(
        functools.partial(rebuild_kernel, n_t, n_b),
        out_shape=(
            jax.ShapeDtypeStruct((n_t, subspaces * sub, columns), BF16),
            jax.ShapeDtypeStruct((n_t, blocks.shape[0], kept, columns), I32),
        ),
        in_specs=[SMEM, SMEM] + [VMEM] * (n_t + n_b),
        out_specs=(VMEM, VMEM),
        scratch_shapes=[
            pltpu.VMEM((n_t, subspaces, columns), I32),
            pltpu.VMEM((subspaces, sub, words), F32),
        ],
        compiler_params=pltpu.CompilerParams(vmem_limit_bytes=(6 + n_t) * MIB),
        cost_estimate=cost(n_t * 10**9, n_t * 2 * 10**6),
    )(place, blocks, *codes, *books)


def main_kernel(n_q, n_w, n_g, woff_ref, tbase_ref, blocks_ref, frow_ref, pos_ref, wt_ref, *refs):
    q_refs, refs = refs[:n_q], refs[n_q:]
    w_refs, refs = refs[:n_w], refs[n_w:]
    g_refs, refs = refs[:n_g], refs[n_g:]
    own_ref, other_ref, grads_refs, refs = refs[0], refs[1], refs[2:-8], refs[-8:]
    w, q, exps, normed, total, gn, nt, some = refs
    for i, w_ref in enumerate(w_refs):
        blocks, rows = w_ref.shape[0], w_ref.shape[1]
        for k in range(blocks):
            w[pl.ds(pl.multiple_of(woff_ref[i * blocks + k], rows), rows), :] = w_ref[k]
    own = q_refs[0].shape[0]
    for i, q_ref in enumerate(q_refs):
        q[i * own : (i + 1) * own, :] = q_ref[...]
    depth = q.shape[1]
    rows = frow_ref.shape[0]
    pick = (frow_ref[...] == lax.broadcasted_iota(I32, (rows, depth), 1)).astype(F32).astype(BF16)
    picked = lax.dot_general(pick, q[...], NT, preferred_element_type=F32).astype(BF16)
    encoded = jnp.dot(q[...], w[...], preferred_element_type=F32)
    inv_rms = lax.rsqrt(jnp.mean(encoded * encoded, axis=1, keepdims=True) + 1e-06)
    normed[...] = encoded * inv_rms
    low = normed[...].astype(BF16)
    q[...] = low
    nt[...] = low.T
    features = grads_refs[0].shape[0]
    for i in range(len(grads_refs)):
        at = pl.ds(pl.multiple_of(blocks_ref[i] * features, features), features)
        some[i * features : (i + 1) * features, :] = nt[at, :]
    total[...] = jnp.zeros_like(total)
    first = 0
    for tiles in g_refs:

        def score(j, _, tiles=tiles, first=first):
            e = jnp.exp(jnp.dot(q[...], tiles[j], preferred_element_type=F32))
            exps[first + j] = e
            total[...] += jnp.sum(e, axis=1, keepdims=True)
            return 0

        lax.fori_loop(0, tiles.shape[0], score, 0)
        first += tiles.shape[0]
    gn[...] = jnp.zeros_like(gn)
    scale = 1.0 / total[...]
    first = 0
    for tiles in g_refs:
        width = tiles.shape[2]

        def back(j, _, tiles=tiles, first=first, width=width):
            ids = tbase_ref[first + j] + lax.broadcasted_iota(I32, (1, width), 1)
            target = (pos_ref[...] == ids).astype(F32)
            gs = (wt_ref[...] * (exps[first + j] * scale - target)).astype(BF16)
            grads = jnp.dot(some[...], gs, preferred_element_type=F32)
            span = pl.ds(pl.multiple_of((first + j) * width, width), width)
            for i, grads_ref in enumerate(grads_refs):
                grads_ref[:, span] = grads[i * features : (i + 1) * features]
            gn[...] += lax.dot_general(gs, tiles[j], NT, preferred_element_type=F32)
            return 0

        lax.fori_loop(0, tiles.shape[0], back, 0)
        first += tiles.shape[0]
    inner = jnp.mean(gn[...] * normed[...], axis=1, keepdims=True)
    grad = (inv_rms * (gn[...] - normed[...] * inner)).astype(BF16)
    half = rows // 2
    own_ref[...] = jnp.dot(picked[:half], grad, preferred_element_type=F32)
    other_ref[...] = jnp.dot(picked[half:], grad, preferred_element_type=F32)


def main(woff, tbase, blocks, rows, frow, pos, wt, q_pieces, w_pieces, groups):
    n_q, n_w, n_g = len(q_pieces), len(w_pieces), len(groups)
    own, depth = q_pieces[0].shape
    queries = own * n_q
    n_t = sum(g.shape[0] for g in groups)
    features, width = groups[0].shape[1:]
    half = frow.shape[0] // 2
    return pl.pallas_call(
        functools.partial(main_kernel, n_q, n_w, n_g),
        out_shape=(jax.ShapeDtypeStruct((half, features), F32),) * 2
        + (jax.ShapeDtypeStruct((rows, n_t * width), F32),) * blocks.shape[0],
        in_specs=[SMEM, SMEM, SMEM, VMEM, VMEM, VMEM] + [VMEM] * (n_q + n_w + n_g),
        out_specs=(VMEM,) * (2 + blocks.shape[0]),
        scratch_shapes=[
            pltpu.VMEM((depth, features), BF16),
            pltpu.VMEM((queries, depth), BF16),
            pltpu.VMEM((n_t, queries, width), F32),
            pltpu.VMEM((queries, features), F32),
            pltpu.VMEM((queries, 1), F32),
            pltpu.VMEM((queries, features), F32),
            pltpu.VMEM((features, queries), BF16),
            pltpu.VMEM((rows * blocks.shape[0], queries), BF16),
        ],
        compiler_params=pltpu.CompilerParams(vmem_limit_bytes=(28 if n_t * queries * width * 4 <= 8 * MIB else 60) * MIB),
        cost_estimate=cost(20 * 10**9, 20 * 10**6),
    )(woff, tbase, blocks, frow, pos, wt, *q_pieces, *w_pieces, *groups)


def words_kernel(words, block, grads_ref, *refs):
    code_refs, (out_ref, codes) = refs[:-2], refs[-2:]
    held, sub = out_ref.shape[0], out_ref.shape[1]
    column = 0
    for code_ref in code_refs:
        width = code_ref.shape[3]
        for j in range(code_ref.shape[0]):
            codes[:, column : column + width] = code_ref[j, block]
            column += width
    low = words // SPLIT
    shift = low.bit_length() - 1
    step = 1024

    def body(group, _):
        code8 = codes[pl.ds(pl.multiple_of(8 * group, 8), 8), :]
        for i in range(8):
            m = 8 * group + i
            grad = grads_ref[pl.ds(pl.multiple_of(sub * m, sub), sub), :]
            upper = grad.astype(BF16).astype(F32)
            parts = jnp.concatenate([upper, grad - upper], 0)
            row = code8[i : i + 1, :]
            acc = None
            for t in range(0, codes.shape[1], step):
                c = row[:, t : t + step]
                p = parts[:, t : t + step]
                high = jnp.broadcast_to(lax.shift_right_logical(c, shift), p.shape)
                p = jnp.concatenate([jnp.where(high == h, p, 0.0) for h in range(SPLIT)], 0)
                hot = (c & (low - 1)) == lax.broadcasted_iota(I32, (low, step), 0)
                r = lax.dot_general(
                    hot.astype(F32).astype(BF16), p.astype(BF16), NT, preferred_element_type=F32
                )
                acc = r if acc is None else acc + r
            acc = acc.T
            pieces = []
            for h in range(SPLIT):
                a = acc[2 * sub * h : 2 * sub * h + sub]
                pieces.append(a + acc[2 * sub * h + sub : 2 * sub * (h + 1)])
            out_ref[m] = jnp.concatenate(pieces, 1)
        return 0

    lax.fori_loop(0, held // 8, body, 0)


def word_grads(block, held, words, grads, codes):
    columns = grads.shape[1]
    sub = grads.shape[0] // held
    return pl.pallas_call(
        functools.partial(words_kernel, words, block),
        out_shape=jax.ShapeDtypeStruct((held, sub, words), F32),
        in_specs=[VMEM] * (1 + len(codes)),
        out_specs=VMEM,
        scratch_shapes=[pltpu.VMEM((held, columns), I32)],
        compiler_params=pltpu.CompilerParams(vmem_limit_bytes=8 * MIB),
        cost_estimate=cost(3 * 10**9, 4 * 10**6),
    )(grads, *codes)


def compute(n_dom, n_sh, n_dp, queries_in, encoder_weight, codebook, codes, positive_ids, loss_weight):
    dom, z, x = (lax.axis_index(a) for a in ("dom", "shard", "dp"))
    n_dev = n_dom * n_sh * n_dp
    group = min(n_sh, 4)
    n_zp, zp, zi = n_sh // group, z // group, lax.rem(z, group)
    evens = range(0, n_dom, 2)
    shards = [lax.rem(z - k + n_sh, n_sh) for k in range(n_sh)]
    lanes = [lax.rem(x - t + n_dp, n_dp) for t in range(n_dp)]
    move = lax.ppermute

    w_rows, depth = encoder_weight.shape
    w_z = jnp.stack([encoder_weight] + [move(encoder_weight, "shard", ring(n_sh, k)) for k in range(1, n_sh)])

    book = codebook[0].astype(BF16)
    words = book.shape[2]
    held_words = book.shape[0] // n_dp
    book_share = [lax.dynamic_slice_in_dim(book, lanes[t] * held_words, held_words, 0) for t in range(n_dp)]
    moved = [move(book_share[0], "shard", ring(n_sh, k)) for k in range(1, n_sh)]
    books = [book_share[0]] + moved
    moved = jnp.concatenate(moved)
    for t in range(1, n_dp):
        books += [book_share[t]] + jnp.split(move(moved, "dp", ring(n_dp, t)), n_sh - 1)
    place = jnp.stack([shards[k] * n_dp + lanes[t] for t in range(n_dp) for k in range(n_sh)]).astype(I32)

    codes_t = codes[0].T.astype(BF16)
    subspaces, pass_rows = codes_t.shape
    width = pass_rows // n_dp
    share = [lax.dynamic_slice_in_dim(codes_t, lanes[t] * width, width, 1) for t in range(n_dp)]
    tiles = {(0, 0): share[0]}
    for k in range(1, n_sh):
        tiles[0, k] = move(share[0], "shard", ring(n_sh, k))
    for t in range(1, n_dp):
        tiles[t, 0] = share[t]
        for k in range(1, n_sh):
            tiles[t, k] = move(tiles[0, k], "dp", ring(n_dp, t))

    q = queries_in[0]
    own = q.shape[0]
    q_pieces = [q] + [move(q, "shard", flip(n_sh, a)) for a in range(1, group)]
    q_from = [(z ^ a) * n_dp + x for a in range(group)]

    w_x = [w_z] + [move(w_z, "dp", ring(n_dp, t)) for t in range(1, n_dp)]
    w_pieces, w_places = [], []
    for e in evens:
        for t in range(n_dp):
            w_pieces.append(w_x[t] if e == 0 else move(w_x[t], "dom", flip(n_dom, e)))
    w_pieces += [move(piece, "dom", flip(n_dom, 1)) for piece in w_pieces]
    for core in range(2):
        for e in evens:
            for t in range(n_dp):
                for k in range(n_sh):
                    w_places.append(((dom ^ (e | core)) * n_sh + shards[k]) * n_dp + lanes[t])
    w_places = jnp.stack(w_places).astype(I32)
    if w_rows % 16:
        whole = jnp.concatenate(w_pieces).reshape(n_dev, w_rows, depth)
        order = jnp.zeros((n_dev,), I32).at[w_places].set(jnp.arange(n_dev, dtype=I32))
        w_pieces = [whole[order].reshape(1, n_dev * w_rows, depth)]
        w_offsets = jnp.zeros((1,), I32)
    else:
        w_offsets = w_places * w_rows

    held = subspaces // (n_sh * n_dp)
    owners = []
    for j in range(n_zp):
        for t in range(n_dp):
            owners.append((lax.rem(zp + j, n_zp) * group + zi) * n_dp + lax.rem(x + t, n_dp))
    blocks = jnp.stack(owners).astype(I32)

    order = [[(t, 0) for t in range(n_dp)]] + [[(t, k) for k in range(1, n_sh)] for t in range(n_dp)]
    bases = [shards[k] * pass_rows + lanes[t] * width for part in order for t, k in part]
    built = []
    for part in order:
        built.append(rebuild(place, blocks, held, [tiles[key] for key in part], books))
    passages = [b[0] for b in built]
    tile_codes = [b[1] for b in built]

    def rows_of(array):
        return jnp.concatenate([lax.dynamic_slice_in_dim(array, f * own, own, 0) for f in q_from])[:, None]

    out_rows = depth // n_dev
    firsts = []
    for core in range(2):
        for e in evens:
            for owner in owners:
                firsts.append(((dom ^ (e | core)) * n_sh * n_dp + owner) * out_rows)
    frow = (jnp.stack(firsts).astype(I32)[:, None] + jnp.arange(out_rows, dtype=I32)[None, :]).reshape(-1, 1)

    own_part, other_part, *grads = main(
        w_offsets,
        jnp.stack(bases).astype(I32),
        blocks,
        held * (depth // subspaces),
        frow,
        rows_of(positive_ids[0]),
        rows_of(loss_weight[0].astype(F32)),
        q_pieces,
        w_pieces,
        passages,
    )

    summed = own_part + move(other_part, "dom", flip(n_dom, 1))
    summed = summed.reshape(len(evens), len(owners), out_rows, depth)
    weight_grad = summed[0, 0]
    book_grad = None
    for o in reversed(range(len(owners))):
        j, t = o // n_dp, o % n_dp
        part = word_grads(o, held, words, grads[o], tile_codes)
        if o:
            pairs = []
            for s in range(n_sh):
                for d in range(n_dp):
                    pairs.append((s * n_dp + d, (s + group * j) % n_sh * n_dp + (d + t) % n_dp))
            part = move(part, ("shard", "dp"), pairs)
        book_grad = part if book_grad is None else book_grad + part
    for i, e in enumerate(evens):
        for o in range(len(owners)):
            if i == o == 0:
                continue
            j, t = o // n_dp, o % n_dp
            pairs = []
            for d in range(n_dom):
                for s in range(n_sh):
                    for c in range(n_dp):
                        to = ((d ^ e) * n_sh + (s + group * j) % n_sh) * n_dp + (c + t) % n_dp
                        pairs.append(((d * n_sh + s) * n_dp + c, to))
            moved = move(summed[i, o], ("dom", "shard", "dp"), pairs)
            weight_grad = weight_grad + moved
    return (weight_grad, book_grad[None])


def solution(mesh):
    sizes = [mesh.shape[a] for a in ("dom", "shard", "dp")]
    return jax.shard_map(
        functools.partial(compute, *sizes),
        mesh=mesh,
        in_specs=(
            P("dom", ("shard", "dp"), None),
            P(("dom", "shard", "dp"), None),
            P("dom", "shard", None, None),
            P("dom", "shard", None),
            P("dom", None),
            P("dom", None),
        ),
        out_specs=(P(("dom", "shard", "dp"), None), P("dom", ("shard", "dp"), None, None)),
        check_vma=False,
    )
```

```python
import functools
import jax
import jax.numpy as jnp
from jax import lax
from jax.experimental import pallas as pl
from jax.experimental.pallas import tpu as pltpu
from jax.sharding import PartitionSpec as P


BF16, F32, I32 = jnp.bfloat16, jnp.float32, jnp.int32
NT = (((1,), (1,)), ((), ()))
LANES = 128
SPLIT = 4
ANY = pl.BlockSpec(memory_space=pl.ANY)
VMEM = pl.BlockSpec(memory_space=pltpu.VMEM)
SMEM = pl.BlockSpec(memory_space=pltpu.SMEM)
SPAN = 32
MIB = 2**20


def ring(n, k):
    return [(i, (i + k) % n) for i in range(n)]


def flip(n, k):
    return [(i, i ^ k) for i in range(n)]


def cost(flops, bytes_accessed):
    return pl.CostEstimate(flops=flops, bytes_accessed=bytes_accessed, transcendentals=0)


def rebuild_kernel(n_t, n_b, place_ref, blocks_ref, *refs):
    code_refs, books = refs[:n_t], refs[n_t : n_t + n_b]
    out_ref, kept_ref, codes_ref, table = refs[n_t + n_b :]
    held, sub, words = books[0].shape
    columns = code_refs[0].shape[1]
    kept = kept_ref.shape[2]
    for i, code_ref in enumerate(code_refs):
        codes_ref[i] = code_ref[...].astype(I32)
        for b in range(kept_ref.shape[1]):
            kept_ref[i, b] = codes_ref[i, pl.ds(pl.multiple_of(blocks_ref[b] * kept, kept), kept), :]
    for piece, book_ref in enumerate(books):
        table[pl.ds(place_ref[piece] * held, held)] = book_ref[...].astype(F32)

    subspaces = code_refs[0].shape[0]
    span = min(subspaces, SPAN)
    steps = subspaces // span

    def body(i, _):
        tile, first = i // steps, lax.rem(i, steps) * span
        for j in range(span // 8):
            rows = pl.multiple_of(first + 8 * j, 8)
            codes = codes_ref[tile, pl.ds(rows, 8), :]
            for pair in range(4):
                tables = []
                for h in range(2):
                    words_of = table[rows + 2 * pair + h]
                    tables.append([words_of[:, c : c + LANES] for c in range(0, words, LANES)])
                for t in range(0, columns, LANES):
                    parts = []
                    for h in range(2):
                        row = codes[2 * pair + h : 2 * pair + h + 1, t : t + LANES]
                        index = jnp.broadcast_to(row, (sub, LANES))
                        lane = index & (LANES - 1)
                        value = None
                        for c, part in enumerate(tables[h]):
                            found = jnp.take_along_axis(part, lane, axis=1, mode="promise_in_bounds")
                            value = found if value is None else jnp.where(index < c * LANES, value, found)
                        parts.append(value)
                    out_rows = pl.ds(pl.multiple_of((rows + 2 * pair) * sub, 2 * sub), 2 * sub)
                    out_ref[tile, out_rows, t : t + LANES] = jnp.concatenate(parts, 0).astype(BF16)
        return 0

    lax.fori_loop(0, n_t * steps, body, 0)


def rebuild(place, blocks, kept, codes, books):
    n_t, n_b = len(codes), len(books)
    subspaces, columns = codes[0].shape
    _, sub, words = books[0].shape
    return pl.pallas_call(
        functools.partial(rebuild_kernel, n_t, n_b),
        out_shape=(
            jax.ShapeDtypeStruct((n_t, subspaces * sub, columns), BF16),
            jax.ShapeDtypeStruct((n_t, blocks.shape[0], kept, columns), I32),
        ),
        in_specs=[SMEM, SMEM] + [VMEM] * (n_t + n_b),
        out_specs=(VMEM, VMEM),
        scratch_shapes=[
            pltpu.VMEM((n_t, subspaces, columns), I32),
            pltpu.VMEM((subspaces, sub, words), F32),
        ],
        compiler_params=pltpu.CompilerParams(vmem_limit_bytes=(6 + n_t) * MIB),
        cost_estimate=cost(n_t * 10**9, n_t * 2 * 10**6),
    )(place, blocks, *codes, *books)


def main_kernel(n_q, n_w, n_g, woff_ref, tbase_ref, blocks_ref, frow_ref, pos_ref, wt_ref, *refs):
    q_refs, refs = refs[:n_q], refs[n_q:]
    w_refs, refs = refs[:n_w], refs[n_w:]
    g_refs, refs = refs[:n_g], refs[n_g:]
    own_ref, other_ref, grads_refs, refs = refs[0], refs[1], refs[2:-8], refs[-8:]
    w, q, exps, normed, total, gn, nt, some = refs
    for i, w_ref in enumerate(w_refs):
        blocks, rows = w_ref.shape[0], w_ref.shape[1]
        for k in range(blocks):
            w[pl.ds(pl.multiple_of(woff_ref[i * blocks + k], rows), rows), :] = w_ref[k]
    own = q_refs[0].shape[0]
    for i, q_ref in enumerate(q_refs):
        q[i * own : (i + 1) * own, :] = q_ref[...]
    depth = q.shape[1]
    rows = frow_ref.shape[0]
    pick = (frow_ref[...] == lax.broadcasted_iota(I32, (rows, depth), 1)).astype(F32).astype(BF16)
    picked = lax.dot_general(pick, q[...], NT, preferred_element_type=F32).astype(BF16)
    encoded = jnp.dot(q[...], w[...], preferred_element_type=F32)
    inv_rms = lax.rsqrt(jnp.mean(encoded * encoded, axis=1, keepdims=True) + 1e-06)
    normed[...] = encoded * inv_rms
    low = normed[...].astype(BF16)
    q[...] = low
    nt[...] = low.T
    features = grads_refs[0].shape[0]
    for i in range(len(grads_refs)):
        at = pl.ds(pl.multiple_of(blocks_ref[i] * features, features), features)
        some[i * features : (i + 1) * features, :] = nt[at, :]
    total[...] = jnp.zeros_like(total)
    first = 0
    for tiles in g_refs:

        def score(j, _, tiles=tiles, first=first):
            e = jnp.exp(jnp.dot(q[...], tiles[j], preferred_element_type=F32))
            exps[first + j] = e
            part = total[...]
            for c in range(0, e.shape[1], LANES):
                part = part + e[:, c : c + LANES]
            total[...] = part
            return 0

        lax.fori_loop(0, tiles.shape[0], score, 0)
        first += tiles.shape[0]
    gn[...] = jnp.zeros_like(gn)
    scale = 1.0 / jnp.sum(total[...], axis=1, keepdims=True)
    first = 0
    for tiles in g_refs:
        width = tiles.shape[2]

        def back(j, _, tiles=tiles, first=first, width=width):
            ids = tbase_ref[first + j] + lax.broadcasted_iota(I32, (1, width), 1)
            target = (pos_ref[...] == ids).astype(F32)
            gs = (wt_ref[...] * (exps[first + j] * scale - target)).astype(BF16)
            grads = jnp.dot(some[...], gs, preferred_element_type=F32)
            span = pl.ds(pl.multiple_of((first + j) * width, width), width)
            for i, grads_ref in enumerate(grads_refs):
                grads_ref[:, span] = grads[i * features : (i + 1) * features]
            gn[...] += lax.dot_general(gs, tiles[j], NT, preferred_element_type=F32)
            return 0

        lax.fori_loop(0, tiles.shape[0], back, 0)
        first += tiles.shape[0]
    inner = jnp.mean(gn[...] * normed[...], axis=1, keepdims=True)
    grad = (inv_rms * (gn[...] - normed[...] * inner)).astype(BF16)
    half = rows // 2
    own_ref[...] = jnp.dot(picked[:half], grad, preferred_element_type=F32)
    other_ref[...] = jnp.dot(picked[half:], grad, preferred_element_type=F32)


def main(woff, tbase, blocks, rows, frow, pos, wt, q_pieces, w_pieces, groups):
    n_q, n_w, n_g = len(q_pieces), len(w_pieces), len(groups)
    own, depth = q_pieces[0].shape
    queries = own * n_q
    n_t = sum(g.shape[0] for g in groups)
    features, width = groups[0].shape[1:]
    half = frow.shape[0] // 2
    return pl.pallas_call(
        functools.partial(main_kernel, n_q, n_w, n_g),
        out_shape=(jax.ShapeDtypeStruct((half, features), F32),) * 2
        + (jax.ShapeDtypeStruct((rows, n_t * width), F32),) * blocks.shape[0],
        in_specs=[SMEM, SMEM, SMEM, VMEM, VMEM, VMEM] + [VMEM] * (n_q + n_w + n_g),
        out_specs=(VMEM,) * (2 + blocks.shape[0]),
        scratch_shapes=[
            pltpu.VMEM((depth, features), BF16),
            pltpu.VMEM((queries, depth), BF16),
            pltpu.VMEM((n_t, queries, width), F32),
            pltpu.VMEM((queries, features), F32),
            pltpu.VMEM((queries, LANES), F32),
            pltpu.VMEM((queries, features), F32),
            pltpu.VMEM((features, queries), BF16),
            pltpu.VMEM((rows * blocks.shape[0], queries), BF16),
        ],
        compiler_params=pltpu.CompilerParams(vmem_limit_bytes=(28 if n_t * queries * width * 4 <= 8 * MIB else 60) * MIB),
        cost_estimate=cost(20 * 10**9, 20 * 10**6),
    )(woff, tbase, blocks, frow, pos, wt, *q_pieces, *w_pieces, *groups)


def words_kernel(words, block, grads_ref, *refs):
    code_refs, (out_ref, codes) = refs[:-2], refs[-2:]
    held, sub = out_ref.shape[0], out_ref.shape[1]
    column = 0
    for code_ref in code_refs:
        width = code_ref.shape[3]
        for j in range(code_ref.shape[0]):
            codes[:, column : column + width] = code_ref[j, block]
            column += width
    low = words // SPLIT
    shift = low.bit_length() - 1
    step = 1024

    def body(group, _):
        code8 = codes[pl.ds(pl.multiple_of(8 * group, 8), 8), :]
        for i in range(8):
            m = 8 * group + i
            grad = grads_ref[pl.ds(pl.multiple_of(sub * m, sub), sub), :]
            upper = grad.astype(BF16).astype(F32)
            parts = jnp.concatenate([upper, grad - upper], 0)
            row = code8[i : i + 1, :]
            acc = None
            for t in range(0, codes.shape[1], step):
                c = row[:, t : t + step]
                p = parts[:, t : t + step]
                high = jnp.broadcast_to(lax.shift_right_logical(c, shift), p.shape)
                p = jnp.concatenate([jnp.where(high == h, p, 0.0) for h in range(SPLIT)], 0)
                hot = (c & (low - 1)) == lax.broadcasted_iota(I32, (low, step), 0)
                r = lax.dot_general(
                    hot.astype(F32).astype(BF16), p.astype(BF16), NT, preferred_element_type=F32
                )
                acc = r if acc is None else acc + r
            acc = acc.T
            pieces = []
            for h in range(SPLIT):
                a = acc[2 * sub * h : 2 * sub * h + sub]
                pieces.append(a + acc[2 * sub * h + sub : 2 * sub * (h + 1)])
            out_ref[m] = jnp.concatenate(pieces, 1)
        return 0

    lax.fori_loop(0, held // 8, body, 0)


def word_grads(block, held, words, grads, codes):
    columns = grads.shape[1]
    sub = grads.shape[0] // held
    return pl.pallas_call(
        functools.partial(words_kernel, words, block),
        out_shape=jax.ShapeDtypeStruct((held, sub, words), F32),
        in_specs=[VMEM] * (1 + len(codes)),
        out_specs=VMEM,
        scratch_shapes=[pltpu.VMEM((held, columns), I32)],
        compiler_params=pltpu.CompilerParams(vmem_limit_bytes=8 * MIB),
        cost_estimate=cost(3 * 10**9, 4 * 10**6),
    )(grads, *codes)


def compute(n_dom, n_sh, n_dp, queries_in, encoder_weight, codebook, codes, positive_ids, loss_weight):
    dom, z, x = (lax.axis_index(a) for a in ("dom", "shard", "dp"))
    n_dev = n_dom * n_sh * n_dp
    group = min(n_sh, 4)
    n_zp, zp, zi = n_sh // group, z // group, lax.rem(z, group)
    evens = range(0, n_dom, 2)
    shards = [lax.rem(z - k + n_sh, n_sh) for k in range(n_sh)]
    lanes = [lax.rem(x - t + n_dp, n_dp) for t in range(n_dp)]
    move = lax.ppermute

    w_rows, depth = encoder_weight.shape
    w_z = jnp.stack([encoder_weight] + [move(encoder_weight, "shard", ring(n_sh, k)) for k in range(1, n_sh)])

    book = codebook[0].astype(BF16)
    words = book.shape[2]
    held_words = book.shape[0] // n_dp
    book_share = [lax.dynamic_slice_in_dim(book, lanes[t] * held_words, held_words, 0) for t in range(n_dp)]
    moved = [move(book_share[0], "shard", ring(n_sh, k)) for k in range(1, n_sh)]
    books = [book_share[0]] + moved
    moved = jnp.concatenate(moved)
    for t in range(1, n_dp):
        across = move(moved, "dp", ring(n_dp, t))
        books += [book_share[t]] + jnp.split(across, n_sh - 1)
    place = jnp.stack([shards[k] * n_dp + lanes[t] for t in range(n_dp) for k in range(n_sh)]).astype(I32)

    codes_t = codes[0].T.astype(BF16)
    subspaces, pass_rows = codes_t.shape
    width = pass_rows // n_dp
    share = [lax.dynamic_slice_in_dim(codes_t, lanes[t] * width, width, 1) for t in range(n_dp)]
    tiles = {(0, 0): share[0]}
    for k in range(1, n_sh):
        tiles[0, k] = move(share[0], "shard", ring(n_sh, k))
    for t in range(1, n_dp):
        tiles[t, 0] = share[t]
        for k in range(1, n_sh):
            tiles[t, k] = move(tiles[0, k], "dp", ring(n_dp, t))

    q = queries_in[0]
    own = q.shape[0]
    q_pieces = [q] + [move(q, "shard", flip(n_sh, a)) for a in range(1, group)]
    q_from = [(z ^ a) * n_dp + x for a in range(group)]

    w_pieces, w_places = [], []
    for e in evens:
        for t in range(n_dp):
            pairs = []
            for d in range(n_dom):
                for c in range(n_dp):
                    pairs.append((d * n_dp + c, (d ^ e) * n_dp + (c + t) % n_dp))
            w_pieces.append(w_z if e == t == 0 else move(w_z, ("dom", "dp"), pairs))
    w_pieces += [move(piece, "dom", flip(n_dom, 1)) for piece in w_pieces]
    for core in range(2):
        for e in evens:
            for t in range(n_dp):
                for k in range(n_sh):
                    w_places.append(((dom ^ (e | core)) * n_sh + shards[k]) * n_dp + lanes[t])
    w_places = jnp.stack(w_places).astype(I32)
    if w_rows % 16:
        whole = jnp.concatenate(w_pieces).reshape(n_dev, w_rows, depth)
        order = jnp.zeros((n_dev,), I32).at[w_places].set(jnp.arange(n_dev, dtype=I32))
        w_pieces = [whole[order].reshape(1, n_dev * w_rows, depth)]
        w_offsets = jnp.zeros((1,), I32)
    else:
        w_offsets = w_places * w_rows

    held = subspaces // (n_sh * n_dp)
    owners = []
    for j in range(n_zp):
        for t in range(n_dp):
            owners.append((lax.rem(zp + j, n_zp) * group + zi) * n_dp + lax.rem(x + t, n_dp))
    blocks = jnp.stack(owners).astype(I32)

    order = [[(t, 0) for t in range(n_dp)]] + [[(t, k) for k in range(1, n_sh)] for t in range(n_dp)]
    bases = [shards[k] * pass_rows + lanes[t] * width for part in order for t, k in part]
    built = []
    for part in order:
        built.append(rebuild(place, blocks, held, [tiles[key] for key in part], books))
    passages = [b[0] for b in built]
    tile_codes = [b[1] for b in built]

    def rows_of(array):
        return jnp.concatenate([lax.dynamic_slice_in_dim(array, f * own, own, 0) for f in q_from])[:, None]

    out_rows = depth // n_dev
    firsts = []
    for core in range(2):
        for e in evens:
            for owner in owners:
                firsts.append(((dom ^ (e | core)) * n_sh * n_dp + owner) * out_rows)
    frow = (jnp.stack(firsts).astype(I32)[:, None] + jnp.arange(out_rows, dtype=I32)[None, :]).reshape(-1, 1)

    own_part, other_part, *grads = main(
        w_offsets,
        jnp.stack(bases).astype(I32),
        blocks,
        held * (depth // subspaces),
        frow,
        rows_of(positive_ids[0]),
        rows_of(loss_weight[0].astype(F32)),
        q_pieces,
        w_pieces,
        passages,
    )

    summed = own_part + move(other_part, "dom", flip(n_dom, 1))
    summed = summed.reshape(len(evens), len(owners), out_rows, depth)
    weight_grad = summed[0, 0]
    book_grad = None
    for o in reversed(range(len(owners))):
        j, t = o // n_dp, o % n_dp
        part = word_grads(o, held, words, grads[o], tile_codes)
        if o:
            pairs = []
            for s in range(n_sh):
                for d in range(n_dp):
                    pairs.append((s * n_dp + d, (s + group * j) % n_sh * n_dp + (d + t) % n_dp))
            part = move(part, ("shard", "dp"), pairs)
        book_grad = part if book_grad is None else book_grad + part
    for i, e in enumerate(evens):
        for o in range(len(owners)):
            if i == o == 0:
                continue
            j, t = o // n_dp, o % n_dp
            pairs = []
            for d in range(n_dom):
                for s in range(n_sh):
                    for c in range(n_dp):
                        to = ((d ^ e) * n_sh + (s + group * j) % n_sh) * n_dp + (c + t) % n_dp
                        pairs.append(((d * n_sh + s) * n_dp + c, to))
            moved = move(summed[i, o], ("dom", "shard", "dp"), pairs)
            weight_grad = weight_grad + moved
    return (weight_grad, book_grad[None])


def solution(mesh):
    sizes = [mesh.shape[a] for a in ("dom", "shard", "dp")]
    return jax.shard_map(
        functools.partial(compute, *sizes),
        mesh=mesh,
        in_specs=(
            P("dom", ("shard", "dp"), None),
            P(("dom", "shard", "dp"), None),
            P("dom", "shard", None, None),
            P("dom", "shard", None),
            P("dom", None),
            P("dom", None),
        ),
        out_specs=(P(("dom", "shard", "dp"), None), P("dom", ("shard", "dp"), None, None)),
        check_vma=False,
    )
```

```python
import functools
import jax
import jax.numpy as jnp
from jax import lax
from jax.experimental import pallas as pl
from jax.experimental.pallas import tpu as pltpu
from jax.sharding import PartitionSpec as P


BF16, F32, I32 = jnp.bfloat16, jnp.float32, jnp.int32
NT = (((1,), (1,)), ((), ()))
LANES = 128
SPLIT = 4
ANY = pl.BlockSpec(memory_space=pl.ANY)
VMEM = pl.BlockSpec(memory_space=pltpu.VMEM)
SMEM = pl.BlockSpec(memory_space=pltpu.SMEM)
SPAN = 64
MIB = 2**20


def ring(n, k):
    return [(i, (i + k) % n) for i in range(n)]


def flip(n, k):
    return [(i, i ^ k) for i in range(n)]


def cost(flops, bytes_accessed):
    return pl.CostEstimate(flops=flops, bytes_accessed=bytes_accessed, transcendentals=0)


def rebuild_kernel(n_t, n_b, place_ref, blocks_ref, *refs):
    code_refs, books = refs[:n_t], refs[n_t : n_t + n_b]
    out_ref, kept_ref, codes_ref, table = refs[n_t + n_b :]
    sub, words = table.shape[1:]
    columns = code_refs[0].shape[1]
    kept = kept_ref.shape[2]
    for i, code_ref in enumerate(code_refs):
        codes_ref[i] = code_ref[...].astype(I32)
        for b in range(kept_ref.shape[1]):
            kept_ref[i, b] = codes_ref[i, pl.ds(pl.multiple_of(blocks_ref[b] * kept, kept), kept), :]
    for piece, book_ref in enumerate(books):
        some = book_ref.shape[0] // sub
        blocks = book_ref.shape[1] // words
        for c in range(blocks):
            part = book_ref[:, c * words : (c + 1) * words].astype(F32).reshape(some, sub, words)
            table[pl.ds((place_ref[piece] * blocks + c) * some, some)] = part

    subspaces = code_refs[0].shape[0]
    span = min(subspaces, SPAN)
    steps = subspaces // span

    def body(i, _):
        tile, first = i // steps, lax.rem(i, steps) * span
        for j in range(span // 8):
            rows = pl.multiple_of(first + 8 * j, 8)
            codes = codes_ref[tile, pl.ds(rows, 8), :]
            for pair in range(4):
                tables = []
                for h in range(2):
                    words_of = table[rows + 2 * pair + h]
                    tables.append([words_of[:, c : c + LANES] for c in range(0, words, LANES)])
                for t in range(0, columns, LANES):
                    parts = []
                    for h in range(2):
                        row = codes[2 * pair + h : 2 * pair + h + 1, t : t + LANES]
                        index = jnp.broadcast_to(row, (sub, LANES))
                        lane = index & (LANES - 1)
                        value = None
                        for c, part in enumerate(tables[h]):
                            found = jnp.take_along_axis(part, lane, axis=1, mode="promise_in_bounds")
                            value = found if value is None else jnp.where(index < c * LANES, value, found)
                        parts.append(value)
                    out_rows = pl.ds(pl.multiple_of((rows + 2 * pair) * sub, 2 * sub), 2 * sub)
                    out_ref[tile, out_rows, t : t + LANES] = jnp.concatenate(parts, 0).astype(BF16)
        return 0

    lax.fori_loop(0, n_t * steps, body, 0)


def rebuild(place, blocks, kept, sub, words, codes, books):
    n_t, n_b = len(codes), len(books)
    subspaces, columns = codes[0].shape
    return pl.pallas_call(
        functools.partial(rebuild_kernel, n_t, n_b),
        out_shape=(
            jax.ShapeDtypeStruct((n_t, subspaces * sub, columns), BF16),
            jax.ShapeDtypeStruct((n_t, blocks.shape[0], kept, columns), I32),
        ),
        in_specs=[SMEM, SMEM] + [VMEM] * (n_t + n_b),
        out_specs=(VMEM, VMEM),
        scratch_shapes=[
            pltpu.VMEM((n_t, subspaces, columns), I32),
            pltpu.VMEM((subspaces, sub, words), F32),
        ],
        compiler_params=pltpu.CompilerParams(vmem_limit_bytes=(6 + n_t) * MIB),
        cost_estimate=cost(n_t * 10**9, n_t * 2 * 10**6),
    )(place, blocks, *codes, *books)


def main_kernel(n_q, n_w, n_g, woff_ref, tbase_ref, blocks_ref, frow_ref, pos_ref, wt_ref, *refs):
    q_refs, refs = refs[:n_q], refs[n_q:]
    w_refs, refs = refs[:n_w], refs[n_w:]
    g_refs, refs = refs[:n_g], refs[n_g:]
    own_ref, other_ref, grads_refs, refs = refs[0], refs[1], refs[2:-8], refs[-8:]
    w, q, exps, normed, total, gn, nt, some = refs
    for i, w_ref in enumerate(w_refs):
        blocks, rows = w_ref.shape[0], w_ref.shape[1]
        for k in range(blocks):
            w[pl.ds(pl.multiple_of(woff_ref[i * blocks + k], rows), rows), :] = w_ref[k]
    own = q_refs[0].shape[0]
    for i, q_ref in enumerate(q_refs):
        q[i * own : (i + 1) * own, :] = q_ref[...]
    depth = q.shape[1]
    rows = frow_ref.shape[0]
    pick = (frow_ref[...] == lax.broadcasted_iota(I32, (rows, depth), 1)).astype(F32).astype(BF16)
    picked = lax.dot_general(pick, q[...], NT, preferred_element_type=F32).astype(BF16)
    encoded = jnp.dot(q[...], w[...], preferred_element_type=F32)
    inv_rms = lax.rsqrt(jnp.mean(encoded * encoded, axis=1, keepdims=True) + 1e-06)
    normed[...] = encoded * inv_rms
    low = normed[...].astype(BF16)
    q[...] = low
    nt[...] = low.T
    features = grads_refs[0].shape[0]
    for i in range(len(grads_refs)):
        at = pl.ds(pl.multiple_of(blocks_ref[i] * features, features), features)
        some[i * features : (i + 1) * features, :] = nt[at, :]
    total[...] = jnp.zeros_like(total)
    first = 0
    for tiles in g_refs:

        def score(j, _, tiles=tiles, first=first):
            e = jnp.exp(jnp.dot(q[...], tiles[j], preferred_element_type=F32))
            exps[first + j] = e
            part = total[...]
            for c in range(0, e.shape[1], LANES):
                part = part + e[:, c : c + LANES]
            total[...] = part
            return 0

        lax.fori_loop(0, tiles.shape[0], score, 0)
        first += tiles.shape[0]
    gn[...] = jnp.zeros_like(gn)
    scale = 1.0 / jnp.sum(total[...], axis=1, keepdims=True)
    first = 0
    for tiles in g_refs:
        width = tiles.shape[2]

        def back(j, _, tiles=tiles, first=first, width=width):
            ids = tbase_ref[first + j] + lax.broadcasted_iota(I32, (1, width), 1)
            target = (pos_ref[...] == ids).astype(F32)
            gs = (wt_ref[...] * (exps[first + j] * scale - target)).astype(BF16)
            grads = jnp.dot(some[...], gs, preferred_element_type=F32)
            span = pl.ds(pl.multiple_of((first + j) * width, width), width)
            for i, grads_ref in enumerate(grads_refs):
                grads_ref[:, span] = grads[i * features : (i + 1) * features]
            gn[...] += lax.dot_general(gs, tiles[j], NT, preferred_element_type=F32)
            return 0

        lax.fori_loop(0, tiles.shape[0], back, 0)
        first += tiles.shape[0]
    inner = jnp.mean(gn[...] * normed[...], axis=1, keepdims=True)
    grad = (inv_rms * (gn[...] - normed[...] * inner)).astype(BF16)
    half = rows // 2
    own_ref[...] = jnp.dot(picked[:half], grad, preferred_element_type=F32)
    other_ref[...] = jnp.dot(picked[half:], grad, preferred_element_type=F32)


def main(woff, tbase, blocks, rows, frow, pos, wt, q_pieces, w_pieces, groups):
    n_q, n_w, n_g = len(q_pieces), len(w_pieces), len(groups)
    own, depth = q_pieces[0].shape
    queries = own * n_q
    n_t = sum(g.shape[0] for g in groups)
    features, width = groups[0].shape[1:]
    half = frow.shape[0] // 2
    return pl.pallas_call(
        functools.partial(main_kernel, n_q, n_w, n_g),
        out_shape=(jax.ShapeDtypeStruct((half, features), F32),) * 2
        + (jax.ShapeDtypeStruct((rows, n_t * width), F32),) * blocks.shape[0],
        in_specs=[SMEM, SMEM, SMEM, VMEM, VMEM, VMEM] + [VMEM] * (n_q + n_w + n_g),
        out_specs=(VMEM,) * (2 + blocks.shape[0]),
        scratch_shapes=[
            pltpu.VMEM((depth, features), BF16),
            pltpu.VMEM((queries, depth), BF16),
            pltpu.VMEM((n_t, queries, width), F32),
            pltpu.VMEM((queries, features), F32),
            pltpu.VMEM((queries, LANES), F32),
            pltpu.VMEM((queries, features), F32),
            pltpu.VMEM((features, queries), BF16),
            pltpu.VMEM((rows * blocks.shape[0], queries), BF16),
        ],
        compiler_params=pltpu.CompilerParams(vmem_limit_bytes=(28 if n_t * queries * width * 4 <= 8 * MIB else 60) * MIB),
        cost_estimate=cost(20 * 10**9, 20 * 10**6),
    )(woff, tbase, blocks, frow, pos, wt, *q_pieces, *w_pieces, *groups)


def words_kernel(words, block, grads_ref, *refs):
    code_refs, (out_ref, codes) = refs[:-2], refs[-2:]
    held, sub = out_ref.shape[0], out_ref.shape[1]
    column = 0
    for code_ref in code_refs:
        width = code_ref.shape[3]
        for j in range(code_ref.shape[0]):
            codes[:, column : column + width] = code_ref[j, block]
            column += width
    low = words // SPLIT
    shift = low.bit_length() - 1
    step = 1024

    def body(group, _):
        code8 = codes[pl.ds(pl.multiple_of(8 * group, 8), 8), :]
        for i in range(8):
            m = 8 * group + i
            grad = grads_ref[pl.ds(pl.multiple_of(sub * m, sub), sub), :]
            upper = grad.astype(BF16).astype(F32)
            parts = jnp.concatenate([upper, grad - upper], 0)
            row = code8[i : i + 1, :]
            acc = None
            for t in range(0, codes.shape[1], step):
                c = row[:, t : t + step]
                p = parts[:, t : t + step]
                high = jnp.broadcast_to(lax.shift_right_logical(c, shift), p.shape)
                p = jnp.concatenate([jnp.where(high == h, p, 0.0) for h in range(SPLIT)], 0)
                hot = (c & (low - 1)) == lax.broadcasted_iota(I32, (low, step), 0)
                r = lax.dot_general(
                    hot.astype(F32).astype(BF16), p.astype(BF16), NT, preferred_element_type=F32
                )
                acc = r if acc is None else acc + r
            acc = acc.T
            pieces = []
            for h in range(SPLIT):
                a = acc[2 * sub * h : 2 * sub * h + sub]
                pieces.append(a + acc[2 * sub * h + sub : 2 * sub * (h + 1)])
            out_ref[m] = jnp.concatenate(pieces, 1)
        return 0

    lax.fori_loop(0, held // 8, body, 0)


def word_grads(block, held, words, grads, codes):
    columns = grads.shape[1]
    sub = grads.shape[0] // held
    return pl.pallas_call(
        functools.partial(words_kernel, words, block),
        out_shape=jax.ShapeDtypeStruct((held, sub, words), F32),
        in_specs=[VMEM] * (1 + len(codes)),
        out_specs=VMEM,
        scratch_shapes=[pltpu.VMEM((held, columns), I32)],
        compiler_params=pltpu.CompilerParams(vmem_limit_bytes=8 * MIB),
        cost_estimate=cost(3 * 10**9, 4 * 10**6),
    )(grads, *codes)


def compute(n_dom, n_sh, n_dp, queries_in, encoder_weight, codebook, codes, positive_ids, loss_weight):
    dom, z, x = (lax.axis_index(a) for a in ("dom", "shard", "dp"))
    n_dev = n_dom * n_sh * n_dp
    group = min(n_sh, 4)
    n_zp, zp, zi = n_sh // group, z // group, lax.rem(z, group)
    evens = range(0, n_dom, 2)
    shards = [lax.rem(z - k + n_sh, n_sh) for k in range(n_sh)]
    lanes = [lax.rem(x - t + n_dp, n_dp) for t in range(n_dp)]
    move = lax.ppermute

    w_rows, depth = encoder_weight.shape
    book = codebook[0].astype(BF16)
    words, sub = book.shape[2], book.shape[1]
    held_words = book.shape[0] // n_dp
    columns = depth // words

    def packed(t):
        mine = lax.dynamic_slice_in_dim(book, lanes[t] * held_words, held_words, 0)
        return jnp.concatenate(jnp.split(mine.reshape(held_words * sub, words), columns), 1)

    packs = [packed(t) for t in range(n_dp)]
    packet = jnp.concatenate([encoder_weight, packs[0]])
    moved = [move(packet, "shard", ring(n_sh, k)) for k in range(1, n_sh)]
    w_z = jnp.stack([encoder_weight] + [m[:w_rows] for m in moved])
    moved = jnp.concatenate([m[w_rows:] for m in moved])
    books = [packs[0]] + jnp.split(moved, n_sh - 1)
    for t in range(1, n_dp):
        across = move(moved, "dp", ring(n_dp, t))
        books += [packs[t]] + jnp.split(across, n_sh - 1)
    place = jnp.stack([shards[k] * n_dp + lanes[t] for t in range(n_dp) for k in range(n_sh)]).astype(I32)

    codes_t = codes[0].T.astype(BF16)
    subspaces, pass_rows = codes_t.shape
    width = pass_rows // n_dp
    share = [lax.dynamic_slice_in_dim(codes_t, lanes[t] * width, width, 1) for t in range(n_dp)]
    tiles = {(0, 0): share[0]}
    for k in range(1, n_sh):
        tiles[0, k] = move(share[0], "shard", ring(n_sh, k))
    for t in range(1, n_dp):
        tiles[t, 0] = share[t]
        for k in range(1, n_sh):
            tiles[t, k] = move(tiles[0, k], "dp", ring(n_dp, t))

    q = queries_in[0]
    own = q.shape[0]
    q_pieces = [q] + [move(q, "shard", flip(n_sh, a)) for a in range(1, group)]
    q_from = [(z ^ a) * n_dp + x for a in range(group)]

    w_pieces, w_places = [], []
    for e in evens:
        for t in range(n_dp):
            pairs = []
            for d in range(n_dom):
                for c in range(n_dp):
                    pairs.append((d * n_dp + c, (d ^ e) * n_dp + (c + t) % n_dp))
            w_pieces.append(w_z if e == t == 0 else move(w_z, ("dom", "dp"), pairs))
    w_pieces += [move(piece, "dom", flip(n_dom, 1)) for piece in w_pieces]
    for core in range(2):
        for e in evens:
            for t in range(n_dp):
                for k in range(n_sh):
                    w_places.append(((dom ^ (e | core)) * n_sh + shards[k]) * n_dp + lanes[t])
    w_places = jnp.stack(w_places).astype(I32)
    if w_rows % 16:
        whole = jnp.concatenate(w_pieces).reshape(n_dev, w_rows, depth)
        order = jnp.zeros((n_dev,), I32).at[w_places].set(jnp.arange(n_dev, dtype=I32))
        w_pieces = [whole[order].reshape(1, n_dev * w_rows, depth)]
        w_offsets = jnp.zeros((1,), I32)
    else:
        w_offsets = w_places * w_rows

    held = subspaces // (n_sh * n_dp)
    owners = []
    for j in range(n_zp):
        for t in range(n_dp):
            owners.append((lax.rem(zp + j, n_zp) * group + zi) * n_dp + lax.rem(x + t, n_dp))
    blocks = jnp.stack(owners).astype(I32)

    order = [[(t, 0) for t in range(n_dp)]] + [[(t, k) for k in range(1, n_sh)] for t in range(n_dp)]
    bases = [shards[k] * pass_rows + lanes[t] * width for part in order for t, k in part]
    built = []
    for part in order:
        built.append(rebuild(place, blocks, held, sub, words, [tiles[key] for key in part], books))
    passages = [b[0] for b in built]
    tile_codes = [b[1] for b in built]

    def rows_of(array):
        return jnp.concatenate([lax.dynamic_slice_in_dim(array, f * own, own, 0) for f in q_from])[:, None]

    out_rows = depth // n_dev
    firsts = []
    for core in range(2):
        for e in evens:
            for owner in owners:
                firsts.append(((dom ^ (e | core)) * n_sh * n_dp + owner) * out_rows)
    frow = (jnp.stack(firsts).astype(I32)[:, None] + jnp.arange(out_rows, dtype=I32)[None, :]).reshape(-1, 1)

    own_part, other_part, *grads = main(
        w_offsets,
        jnp.stack(bases).astype(I32),
        blocks,
        held * (depth // subspaces),
        frow,
        rows_of(positive_ids[0]),
        rows_of(loss_weight[0].astype(F32)),
        q_pieces,
        w_pieces,
        passages,
    )

    summed = own_part + move(other_part, "dom", flip(n_dom, 1))
    summed = summed.reshape(len(evens), len(owners), out_rows, depth)
    weight_grad = summed[0, 0]
    book_grad = None
    for o in reversed(range(len(owners))):
        j, t = o // n_dp, o % n_dp
        part = word_grads(o, held, words, grads[o], tile_codes)
        if o:
            pairs = []
            for s in range(n_sh):
                for d in range(n_dp):
                    pairs.append((s * n_dp + d, (s + group * j) % n_sh * n_dp + (d + t) % n_dp))
            part = move(part, ("shard", "dp"), pairs)
        book_grad = part if book_grad is None else book_grad + part
    for i, e in enumerate(evens):
        for o in range(len(owners)):
            if i == o == 0:
                continue
            j, t = o // n_dp, o % n_dp
            pairs = []
            for d in range(n_dom):
                for s in range(n_sh):
                    for c in range(n_dp):
                        to = ((d ^ e) * n_sh + (s + group * j) % n_sh) * n_dp + (c + t) % n_dp
                        pairs.append(((d * n_sh + s) * n_dp + c, to))
            moved = move(summed[i, o], ("dom", "shard", "dp"), pairs)
            weight_grad = weight_grad + moved
    return (weight_grad, book_grad[None])


def solution(mesh):
    sizes = [mesh.shape[a] for a in ("dom", "shard", "dp")]
    return jax.shard_map(
        functools.partial(compute, *sizes),
        mesh=mesh,
        in_specs=(
            P("dom", ("shard", "dp"), None),
            P(("dom", "shard", "dp"), None),
            P("dom", "shard", None, None),
            P("dom", "shard", None),
            P("dom", None),
            P("dom", None),
        ),
        out_specs=(P(("dom", "shard", "dp"), None), P("dom", ("shard", "dp"), None, None)),
        check_vma=False,
    )
```

```python
import functools
import jax
import jax.numpy as jnp
from jax import lax
from jax.experimental import pallas as pl
from jax.experimental.pallas import tpu as pltpu
from jax.sharding import PartitionSpec as P


BF16, F32, I32 = jnp.bfloat16, jnp.float32, jnp.int32
NT = (((1,), (1,)), ((), ()))
LANES = 128
SPLIT = 4
ANY = pl.BlockSpec(memory_space=pl.ANY)
VMEM = pl.BlockSpec(memory_space=pltpu.VMEM)
SMEM = pl.BlockSpec(memory_space=pltpu.SMEM)
SPAN = 64
MIB = 2**20


def ring(n, k):
    return [(i, (i + k) % n) for i in range(n)]


def flip(n, k):
    return [(i, i ^ k) for i in range(n)]


def relay(n):
    return list(range(1, n // 2 + 1)) + list(range(n - 1, n // 2, -1))


def cost(flops, bytes_accessed):
    return pl.CostEstimate(flops=flops, bytes_accessed=bytes_accessed, transcendentals=0)


def rebuild_kernel(n_t, n_b, place_ref, blocks_ref, *refs):
    code_refs, books = refs[:n_t], refs[n_t : n_t + n_b]
    out_ref, kept_ref, codes_ref, table = refs[n_t + n_b :]
    sub, words = table.shape[1:]
    columns = code_refs[0].shape[1]
    kept = kept_ref.shape[2]
    for i, code_ref in enumerate(code_refs):
        codes_ref[i] = code_ref[...].astype(I32)
        for b in range(kept_ref.shape[1]):
            kept_ref[i, b] = codes_ref[i, pl.ds(pl.multiple_of(blocks_ref[b] * kept, kept), kept), :]
    for piece, book_ref in enumerate(books):
        some = book_ref.shape[0] // sub
        blocks = book_ref.shape[1] // words
        for c in range(blocks):
            part = book_ref[:, c * words : (c + 1) * words].astype(F32).reshape(some, sub, words)
            table[pl.ds((place_ref[piece] * blocks + c) * some, some)] = part

    subspaces = code_refs[0].shape[0]
    span = min(subspaces, SPAN)
    steps = subspaces // span

    def body(i, _):
        tile, first = i // steps, lax.rem(i, steps) * span
        for j in range(span // 8):
            rows = pl.multiple_of(first + 8 * j, 8)
            codes = codes_ref[tile, pl.ds(rows, 8), :]
            for pair in range(4):
                tables = []
                for h in range(2):
                    words_of = table[rows + 2 * pair + h]
                    tables.append([words_of[:, c : c + LANES] for c in range(0, words, LANES)])
                for t in range(0, columns, LANES):
                    parts = []
                    for h in range(2):
                        row = codes[2 * pair + h : 2 * pair + h + 1, t : t + LANES]
                        index = jnp.broadcast_to(row, (sub, LANES))
                        lane = index & (LANES - 1)
                        value = None
                        for c, part in enumerate(tables[h]):
                            found = jnp.take_along_axis(part, lane, axis=1, mode="promise_in_bounds")
                            value = found if value is None else jnp.where(index < c * LANES, value, found)
                        parts.append(value)
                    out_rows = pl.ds(pl.multiple_of((rows + 2 * pair) * sub, 2 * sub), 2 * sub)
                    out_ref[tile, out_rows, t : t + LANES] = jnp.concatenate(parts, 0).astype(BF16)
        return 0

    lax.fori_loop(0, n_t * steps, body, 0)


def rebuild(place, blocks, kept, sub, words, codes, books):
    n_t, n_b = len(codes), len(books)
    subspaces, columns = codes[0].shape
    return pl.pallas_call(
        functools.partial(rebuild_kernel, n_t, n_b),
        out_shape=(
            jax.ShapeDtypeStruct((n_t, subspaces * sub, columns), BF16),
            jax.ShapeDtypeStruct((n_t, blocks.shape[0], kept, columns), I32),
        ),
        in_specs=[SMEM, SMEM] + [VMEM] * (n_t + n_b),
        out_specs=(VMEM, VMEM),
        scratch_shapes=[
            pltpu.VMEM((n_t, subspaces, columns), I32),
            pltpu.VMEM((subspaces, sub, words), F32),
        ],
        compiler_params=pltpu.CompilerParams(vmem_limit_bytes=(6 + n_t) * MIB),
        cost_estimate=cost(n_t * 10**9, n_t * 2 * 10**6),
    )(place, blocks, *codes, *books)


def main_kernel(n_q, n_w, n_g, woff_ref, tbase_ref, blocks_ref, frow_ref, pos_ref, wt_ref, *refs):
    q_refs, refs = refs[:n_q], refs[n_q:]
    w_refs, refs = refs[:n_w], refs[n_w:]
    g_refs, refs = refs[:n_g], refs[n_g:]
    own_ref, other_ref, grads_refs, refs = refs[0], refs[1], refs[2:-8], refs[-8:]
    w, q, exps, normed, total, gn, nt, some = refs
    for i, w_ref in enumerate(w_refs):
        blocks, rows = w_ref.shape[0], w_ref.shape[1]
        for k in range(blocks):
            w[pl.ds(pl.multiple_of(woff_ref[i * blocks + k], rows), rows), :] = w_ref[k]
    own = q_refs[0].shape[0]
    for i, q_ref in enumerate(q_refs):
        q[i * own : (i + 1) * own, :] = q_ref[...]
    depth = q.shape[1]
    rows = frow_ref.shape[0]
    pick = (frow_ref[...] == lax.broadcasted_iota(I32, (rows, depth), 1)).astype(F32).astype(BF16)
    picked = lax.dot_general(pick, q[...], NT, preferred_element_type=F32).astype(BF16)
    encoded = jnp.dot(q[...], w[...], preferred_element_type=F32)
    inv_rms = lax.rsqrt(jnp.mean(encoded * encoded, axis=1, keepdims=True) + 1e-06)
    normed[...] = encoded * inv_rms
    low = normed[...].astype(BF16)
    q[...] = low
    nt[...] = low.T
    features = grads_refs[0].shape[0]
    for i in range(len(grads_refs)):
        at = pl.ds(pl.multiple_of(blocks_ref[i] * features, features), features)
        some[i * features : (i + 1) * features, :] = nt[at, :]
    total[...] = jnp.zeros_like(total)
    first = 0
    for tiles in g_refs:

        def score(j, _, tiles=tiles, first=first):
            e = jnp.exp(jnp.dot(q[...], tiles[j], preferred_element_type=F32))
            exps[first + j] = e
            part = total[...]
            for c in range(0, e.shape[1], LANES):
                part = part + e[:, c : c + LANES]
            total[...] = part
            return 0

        lax.fori_loop(0, tiles.shape[0], score, 0)
        first += tiles.shape[0]
    gn[...] = jnp.zeros_like(gn)
    scale = 1.0 / jnp.sum(total[...], axis=1, keepdims=True)
    first = 0
    for tiles in g_refs:
        width = tiles.shape[2]

        def back(j, _, tiles=tiles, first=first, width=width):
            ids = tbase_ref[first + j] + lax.broadcasted_iota(I32, (1, width), 1)
            target = (pos_ref[...] == ids).astype(F32)
            gs = (wt_ref[...] * (exps[first + j] * scale - target)).astype(BF16)
            grads = jnp.dot(some[...], gs, preferred_element_type=F32)
            span = pl.ds(pl.multiple_of((first + j) * width, width), width)
            for i, grads_ref in enumerate(grads_refs):
                grads_ref[:, span] = grads[i * features : (i + 1) * features]
            gn[...] += lax.dot_general(gs, tiles[j], NT, preferred_element_type=F32)
            return 0

        lax.fori_loop(0, tiles.shape[0], back, 0)
        first += tiles.shape[0]
    inner = jnp.mean(gn[...] * normed[...], axis=1, keepdims=True)
    grad = (inv_rms * (gn[...] - normed[...] * inner)).astype(BF16)
    half = rows // 2
    own_ref[...] = jnp.dot(picked[:half], grad, preferred_element_type=F32)
    other_ref[...] = jnp.dot(picked[half:], grad, preferred_element_type=F32)


def main(woff, tbase, blocks, rows, frow, pos, wt, q_pieces, w_pieces, groups):
    n_q, n_w, n_g = len(q_pieces), len(w_pieces), len(groups)
    own, depth = q_pieces[0].shape
    queries = own * n_q
    n_t = sum(g.shape[0] for g in groups)
    features, width = groups[0].shape[1:]
    half = frow.shape[0] // 2
    return pl.pallas_call(
        functools.partial(main_kernel, n_q, n_w, n_g),
        out_shape=(jax.ShapeDtypeStruct((half, features), F32),) * 2
        + (jax.ShapeDtypeStruct((rows, n_t * width), F32),) * blocks.shape[0],
        in_specs=[SMEM, SMEM, SMEM, VMEM, VMEM, VMEM] + [VMEM] * (n_q + n_w + n_g),
        out_specs=(VMEM,) * (2 + blocks.shape[0]),
        scratch_shapes=[
            pltpu.VMEM((depth, features), BF16),
            pltpu.VMEM((queries, depth), BF16),
            pltpu.VMEM((n_t, queries, width), F32),
            pltpu.VMEM((queries, features), F32),
            pltpu.VMEM((queries, LANES), F32),
            pltpu.VMEM((queries, features), F32),
            pltpu.VMEM((features, queries), BF16),
            pltpu.VMEM((rows * blocks.shape[0], queries), BF16),
        ],
        compiler_params=pltpu.CompilerParams(vmem_limit_bytes=(28 if n_t * queries * width * 4 <= 8 * MIB else 60) * MIB),
        cost_estimate=cost(20 * 10**9, 20 * 10**6),
    )(woff, tbase, blocks, frow, pos, wt, *q_pieces, *w_pieces, *groups)


def words_kernel(words, block, grads_ref, *refs):
    code_refs, (out_ref, codes) = refs[:-2], refs[-2:]
    held, sub = out_ref.shape[0], out_ref.shape[1]
    column = 0
    for code_ref in code_refs:
        width = code_ref.shape[3]
        for j in range(code_ref.shape[0]):
            codes[:, column : column + width] = code_ref[j, block]
            column += width
    low = words // SPLIT
    shift = low.bit_length() - 1
    step = 1024

    def body(group, _):
        code8 = codes[pl.ds(pl.multiple_of(8 * group, 8), 8), :]
        for i in range(8):
            m = 8 * group + i
            grad = grads_ref[pl.ds(pl.multiple_of(sub * m, sub), sub), :]
            upper = grad.astype(BF16).astype(F32)
            parts = jnp.concatenate([upper, grad - upper], 0)
            row = code8[i : i + 1, :]
            acc = None
            for t in range(0, codes.shape[1], step):
                c = row[:, t : t + step]
                p = parts[:, t : t + step]
                high = jnp.broadcast_to(lax.shift_right_logical(c, shift), p.shape)
                p = jnp.concatenate([jnp.where(high == h, p, 0.0) for h in range(SPLIT)], 0)
                hot = (c & (low - 1)) == lax.broadcasted_iota(I32, (low, step), 0)
                r = lax.dot_general(
                    hot.astype(F32).astype(BF16), p.astype(BF16), NT, preferred_element_type=F32
                )
                acc = r if acc is None else acc + r
            acc = acc.T
            pieces = []
            for h in range(SPLIT):
                a = acc[2 * sub * h : 2 * sub * h + sub]
                pieces.append(a + acc[2 * sub * h + sub : 2 * sub * (h + 1)])
            out_ref[m] = jnp.concatenate(pieces, 1)
        return 0

    lax.fori_loop(0, held // 8, body, 0)


def word_grads(block, held, words, grads, codes):
    columns = grads.shape[1]
    sub = grads.shape[0] // held
    return pl.pallas_call(
        functools.partial(words_kernel, words, block),
        out_shape=jax.ShapeDtypeStruct((held, sub, words), F32),
        in_specs=[VMEM] * (1 + len(codes)),
        out_specs=VMEM,
        scratch_shapes=[pltpu.VMEM((held, columns), I32)],
        compiler_params=pltpu.CompilerParams(vmem_limit_bytes=8 * MIB),
        cost_estimate=cost(3 * 10**9, 4 * 10**6),
    )(grads, *codes)


def compute(n_dom, n_sh, n_dp, queries_in, encoder_weight, codebook, codes, positive_ids, loss_weight):
    dom, z, x = (lax.axis_index(a) for a in ("dom", "shard", "dp"))
    n_dev = n_dom * n_sh * n_dp
    group = min(n_sh, 4)
    n_zp, zp, zi = n_sh // group, z // group, lax.rem(z, group)
    evens = range(0, n_dom, 2)
    shards = [lax.rem(z - k + n_sh, n_sh) for k in range(n_sh)]
    lanes = [lax.rem(x - t + n_dp, n_dp) for t in range(n_dp)]
    move = lax.ppermute

    w_rows, depth = encoder_weight.shape
    book = codebook[0].astype(BF16)
    words, sub = book.shape[2], book.shape[1]
    held_words = book.shape[0] // n_dp
    columns = depth // words

    def packed(t):
        mine = lax.dynamic_slice_in_dim(book, lanes[t] * held_words, held_words, 0)
        return jnp.concatenate(jnp.split(mine.reshape(held_words * sub, words), columns), 1)

    packs = [packed(t) for t in range(n_dp)]
    packet = jnp.concatenate([encoder_weight, packs[0]])
    moved = [move(packet, "shard", ring(n_sh, k)) for k in range(1, n_sh)]
    w_z = jnp.stack([encoder_weight] + [m[:w_rows] for m in moved])
    moved = jnp.concatenate([m[w_rows:] for m in moved])
    books = [packs[0]] + jnp.split(moved, n_sh - 1)
    for t in range(1, n_dp):
        across = move(moved, "dp", ring(n_dp, t))
        books += [packs[t]] + jnp.split(across, n_sh - 1)
    place = jnp.stack([shards[k] * n_dp + lanes[t] for t in range(n_dp) for k in range(n_sh)]).astype(I32)

    codes_t = codes[0].T.astype(BF16)
    subspaces, pass_rows = codes_t.shape
    width = pass_rows // n_dp
    share = [lax.dynamic_slice_in_dim(codes_t, lanes[t] * width, width, 1) for t in range(n_dp)]
    tiles = {(0, 0): share[0]}
    for k in relay(n_sh):
        step = 1 if 2 * k <= n_sh else n_sh - 1
        source = tiles[0, (k - step) % n_sh]
        tiles[0, k] = move(source, "shard", ring(n_sh, step))
    for t in range(1, n_dp):
        tiles[t, 0] = share[t]
        for k in range(1, n_sh):
            tiles[t, k] = move(tiles[0, k], "dp", ring(n_dp, t))

    q = queries_in[0]
    own = q.shape[0]
    q_held = {0: q}
    for k in relay(group):
        step = 1 if 2 * k <= group else group - 1
        pairs = [(s, s // group * group + (s + step) % group) for s in range(n_sh)]
        q_held[k] = move(q_held[(k - step) % group], "shard", pairs)
    q_pieces = [q_held[k] for k in range(group)]
    q_from = [(zp * group + lax.rem(zi - k + group, group)) * n_dp + x for k in range(group)]

    w_pieces, w_places = [], []
    for e in evens:
        for t in range(n_dp):
            pairs = []
            for d in range(n_dom):
                for c in range(n_dp):
                    pairs.append((d * n_dp + c, (d ^ e) * n_dp + (c + t) % n_dp))
            w_pieces.append(w_z if e == t == 0 else move(w_z, ("dom", "dp"), pairs))
    w_pieces += [move(piece, "dom", flip(n_dom, 1)) for piece in w_pieces]
    for core in range(2):
        for e in evens:
            for t in range(n_dp):
                for k in range(n_sh):
                    w_places.append(((dom ^ (e | core)) * n_sh + shards[k]) * n_dp + lanes[t])
    w_places = jnp.stack(w_places).astype(I32)
    if w_rows % 16:
        whole = jnp.concatenate(w_pieces).reshape(n_dev, w_rows, depth)
        order = jnp.zeros((n_dev,), I32).at[w_places].set(jnp.arange(n_dev, dtype=I32))
        w_pieces = [whole[order].reshape(1, n_dev * w_rows, depth)]
        w_offsets = jnp.zeros((1,), I32)
    else:
        w_offsets = w_places * w_rows

    held = subspaces // (n_sh * n_dp)
    owners = []
    for j in range(n_zp):
        for t in range(n_dp):
            owners.append((lax.rem(zp + j, n_zp) * group + zi) * n_dp + lax.rem(x + t, n_dp))
    blocks = jnp.stack(owners).astype(I32)

    order = [[(t, 0) for t in range(n_dp)]] + [[(t, k) for k in range(1, n_sh)] for t in range(n_dp)]
    bases = [shards[k] * pass_rows + lanes[t] * width for part in order for t, k in part]
    built = []
    for part in order:
        built.append(rebuild(place, blocks, held, sub, words, [tiles[key] for key in part], books))
    passages = [b[0] for b in built]
    tile_codes = [b[1] for b in built]

    def rows_of(array):
        return jnp.concatenate([lax.dynamic_slice_in_dim(array, f * own, own, 0) for f in q_from])[:, None]

    out_rows = depth // n_dev
    firsts = []
    for core in range(2):
        for e in evens:
            for owner in owners:
                firsts.append(((dom ^ (e | core)) * n_sh * n_dp + owner) * out_rows)
    frow = (jnp.stack(firsts).astype(I32)[:, None] + jnp.arange(out_rows, dtype=I32)[None, :]).reshape(-1, 1)

    own_part, other_part, *grads = main(
        w_offsets,
        jnp.stack(bases).astype(I32),
        blocks,
        held * (depth // subspaces),
        frow,
        rows_of(positive_ids[0]),
        rows_of(loss_weight[0].astype(F32)),
        q_pieces,
        w_pieces,
        passages,
    )

    summed = own_part + move(other_part, "dom", flip(n_dom, 1))
    summed = summed.reshape(len(evens), len(owners), out_rows, depth)
    weight_grad = summed[0, 0]
    book_grad = None
    for o in reversed(range(len(owners))):
        j, t = o // n_dp, o % n_dp
        part = word_grads(o, held, words, grads[o], tile_codes)
        if o:
            pairs = []
            for s in range(n_sh):
                for d in range(n_dp):
                    pairs.append((s * n_dp + d, (s + group * j) % n_sh * n_dp + (d + t) % n_dp))
            part = move(part, ("shard", "dp"), pairs)
        book_grad = part if book_grad is None else book_grad + part
    for i, e in enumerate(evens):
        for o in range(len(owners)):
            if i == o == 0:
                continue
            j, t = o // n_dp, o % n_dp
            pairs = []
            for d in range(n_dom):
                for s in range(n_sh):
                    for c in range(n_dp):
                        to = ((d ^ e) * n_sh + (s + group * j) % n_sh) * n_dp + (c + t) % n_dp
                        pairs.append(((d * n_sh + s) * n_dp + c, to))
            moved = move(summed[i, o], ("dom", "shard", "dp"), pairs)
            weight_grad = weight_grad + moved
    return (weight_grad, book_grad[None])


def solution(mesh):
    sizes = [mesh.shape[a] for a in ("dom", "shard", "dp")]
    return jax.shard_map(
        functools.partial(compute, *sizes),
        mesh=mesh,
        in_specs=(
            P("dom", ("shard", "dp"), None),
            P(("dom", "shard", "dp"), None),
            P("dom", "shard", None, None),
            P("dom", "shard", None),
            P("dom", None),
            P("dom", None),
        ),
        out_specs=(P(("dom", "shard", "dp"), None), P("dom", ("shard", "dp"), None, None)),
        check_vma=False,
    )
```

```python
import functools
import jax
import jax.numpy as jnp
from jax import lax
from jax.experimental import pallas as pl
from jax.experimental.pallas import tpu as pltpu
from jax.sharding import PartitionSpec as P


BF16, F32, I32 = jnp.bfloat16, jnp.float32, jnp.int32
NT = (((1,), (1,)), ((), ()))
LANES = 128
SPLIT = 4
ANY = pl.BlockSpec(memory_space=pl.ANY)
VMEM = pl.BlockSpec(memory_space=pltpu.VMEM)
SMEM = pl.BlockSpec(memory_space=pltpu.SMEM)
SPAN = 64
MIB = 2**20


def ring(n, k):
    return [(i, (i + k) % n) for i in range(n)]


def flip(n, k):
    return [(i, i ^ k) for i in range(n)]


def relay(n):
    return list(range(1, n // 2 + 1)) + list(range(n - 1, n // 2, -1))


def cost(flops, bytes_accessed):
    return pl.CostEstimate(flops=flops, bytes_accessed=bytes_accessed, transcendentals=0)


def rebuild_kernel(n_t, n_b, place_ref, blocks_ref, *refs):
    code_refs, books = refs[:n_t], refs[n_t : n_t + n_b]
    out_ref, kept_ref, codes_ref, table = refs[n_t + n_b :]
    sub, words = table.shape[1:]
    columns = code_refs[0].shape[1]
    kept = kept_ref.shape[2]
    for i, code_ref in enumerate(code_refs):
        codes_ref[i] = code_ref[...].astype(I32)
        for b in range(kept_ref.shape[1]):
            kept_ref[i, b] = codes_ref[i, pl.ds(pl.multiple_of(blocks_ref[b] * kept, kept), kept), :]
    for piece, book_ref in enumerate(books):
        some = book_ref.shape[0] // sub
        blocks = book_ref.shape[1] // words
        for c in range(blocks):
            part = book_ref[:, c * words : (c + 1) * words].astype(F32).reshape(some, sub, words)
            table[pl.ds((place_ref[piece] * blocks + c) * some, some)] = part

    subspaces = code_refs[0].shape[0]
    span = min(subspaces, SPAN)
    steps = subspaces // span

    def body(i, _):
        tile, first = i // steps, lax.rem(i, steps) * span
        for j in range(span // 8):
            rows = pl.multiple_of(first + 8 * j, 8)
            codes = codes_ref[tile, pl.ds(rows, 8), :]
            for pair in range(4):
                tables = []
                for h in range(2):
                    words_of = table[rows + 2 * pair + h]
                    tables.append([words_of[:, c : c + LANES] for c in range(0, words, LANES)])
                for t in range(0, columns, LANES):
                    parts = []
                    for h in range(2):
                        row = codes[2 * pair + h : 2 * pair + h + 1, t : t + LANES]
                        index = jnp.broadcast_to(row, (sub, LANES))
                        lane = index & (LANES - 1)
                        value = None
                        for c, part in enumerate(tables[h]):
                            found = jnp.take_along_axis(part, lane, axis=1, mode="promise_in_bounds")
                            value = found if value is None else jnp.where(index < c * LANES, value, found)
                        parts.append(value)
                    out_rows = pl.ds(pl.multiple_of((rows + 2 * pair) * sub, 2 * sub), 2 * sub)
                    out_ref[tile, out_rows, t : t + LANES] = jnp.concatenate(parts, 0).astype(BF16)
        return 0

    lax.fori_loop(0, n_t * steps, body, 0)


def rebuild(place, blocks, kept, sub, words, codes, books):
    n_t, n_b = len(codes), len(books)
    subspaces, columns = codes[0].shape
    return pl.pallas_call(
        functools.partial(rebuild_kernel, n_t, n_b),
        out_shape=(
            jax.ShapeDtypeStruct((n_t, subspaces * sub, columns), BF16),
            jax.ShapeDtypeStruct((n_t, blocks.shape[0], kept, columns), I32),
        ),
        in_specs=[SMEM, SMEM] + [VMEM] * (n_t + n_b),
        out_specs=(VMEM, VMEM),
        scratch_shapes=[
            pltpu.VMEM((n_t, subspaces, columns), I32),
            pltpu.VMEM((subspaces, sub, words), F32),
        ],
        compiler_params=pltpu.CompilerParams(vmem_limit_bytes=(6 + n_t) * MIB),
        cost_estimate=cost(n_t * 10**9, n_t * 2 * 10**6),
    )(place, blocks, *codes, *books)


def main_kernel(n_q, n_w, n_g, woff_ref, tbase_ref, blocks_ref, frow_ref, pos_ref, wt_ref, *refs):
    q_refs, refs = refs[:n_q], refs[n_q:]
    w_refs, refs = refs[:n_w], refs[n_w:]
    g_refs, refs = refs[:n_g], refs[n_g:]
    own_ref, other_ref, grads_refs, refs = refs[0], refs[1], refs[2:-12], refs[-12:]
    w, q, exps, normed, total, gn, nt, some, ahead, places, even, odd = refs
    for i, w_ref in enumerate(w_refs):
        blocks, rows = w_ref.shape[0], w_ref.shape[1]
        for k in range(blocks):
            w[pl.ds(pl.multiple_of(woff_ref[i * blocks + k], rows), rows), :] = w_ref[k]
    own = q_refs[0].shape[0]
    for i, q_ref in enumerate(q_refs):
        q[i * own : (i + 1) * own, :] = q_ref[...]
    depth = q.shape[1]
    rows = frow_ref.shape[0]
    pick = (frow_ref[...] == lax.broadcasted_iota(I32, (rows, depth), 1)).astype(F32).astype(BF16)
    picked = lax.dot_general(pick, q[...], NT, preferred_element_type=F32).astype(BF16)
    encoded = jnp.dot(q[...], w[...], preferred_element_type=F32)
    inv_rms = lax.rsqrt(jnp.mean(encoded * encoded, axis=1, keepdims=True) + 1e-06)
    normed[...] = encoded * inv_rms
    low = normed[...].astype(BF16)
    q[...] = low
    nt[...] = low.T
    features = grads_refs[0].shape[0]
    for i in range(len(grads_refs)):
        at = pl.ds(pl.multiple_of(blocks_ref[i] * features, features), features)
        some[i * features : (i + 1) * features, :] = nt[at, :]
    at = [(tiles, j) for tiles in g_refs for j in range(tiles.shape[0])]
    width = at[0][0].shape[2]
    spread = [pl.ds(c, LANES) for c in range(0, width, LANES)]
    total[...] = jnp.zeros_like(total)

    def exponent(n):
        part = total[...]
        for c in spread:
            e = jnp.exp(exps[n, :, c])
            exps[n, :, c] = e
            part = part + e
        total[...] = part

    for n, (tiles, j) in enumerate(at):
        exps[n] = jnp.dot(q[...], tiles[j], preferred_element_type=F32)
        if n:
            exponent(n - 1)
    exponent(len(at) - 1)
    scale = wt_ref[...] / jnp.sum(total[...], axis=1, keepdims=True)
    ahead[0] = jnp.broadcast_to(scale, total.shape)
    ahead[1] = jnp.broadcast_to(wt_ref[...], total.shape)
    places[...] = jnp.broadcast_to(pos_ref[...], total.shape)
    lane = lax.broadcasted_iota(I32, (1, LANES), 1)

    def weigh(n):
        out = (even, odd)[n % 2]
        for i, c in enumerate(spread):
            hit = places[...] == lane + (tbase_ref[n] + i * LANES)
            out[:, c] = (exps[n, :, c] * ahead[0] - jnp.where(hit, ahead[1], 0.0)).astype(BF16)

    weigh(0)
    for n, (tiles, j) in enumerate(at):
        gs = (even, odd)[n % 2]
        if n + 1 < len(at):
            weigh(n + 1)
        more = lax.dot_general(gs[...], tiles[j], NT, preferred_element_type=F32)
        gn[...] = more if n == 0 else gn[...] + more
        grads = jnp.dot(some[...], gs[...], preferred_element_type=F32)
        for i, grads_ref in enumerate(grads_refs):
            grads_ref[:, n * width : (n + 1) * width] = grads[i * features : (i + 1) * features]
    inner = jnp.mean(gn[...] * normed[...], axis=1, keepdims=True)
    grad = (inv_rms * (gn[...] - normed[...] * inner)).astype(BF16)
    half = rows // 2
    own_ref[...] = jnp.dot(picked[:half], grad, preferred_element_type=F32)
    other_ref[...] = jnp.dot(picked[half:], grad, preferred_element_type=F32)


def main(woff, tbase, blocks, rows, frow, pos, wt, q_pieces, w_pieces, groups):
    n_q, n_w, n_g = len(q_pieces), len(w_pieces), len(groups)
    own, depth = q_pieces[0].shape
    queries = own * n_q
    n_t = sum(g.shape[0] for g in groups)
    features, width = groups[0].shape[1:]
    half = frow.shape[0] // 2
    return pl.pallas_call(
        functools.partial(main_kernel, n_q, n_w, n_g),
        out_shape=(jax.ShapeDtypeStruct((half, features), F32),) * 2
        + (jax.ShapeDtypeStruct((rows, n_t * width), F32),) * blocks.shape[0],
        in_specs=[SMEM, SMEM, SMEM, VMEM, VMEM, VMEM] + [VMEM] * (n_q + n_w + n_g),
        out_specs=(VMEM,) * (2 + blocks.shape[0]),
        scratch_shapes=[
            pltpu.VMEM((depth, features), BF16),
            pltpu.VMEM((queries, depth), BF16),
            pltpu.VMEM((n_t, queries, width), F32),
            pltpu.VMEM((queries, features), F32),
            pltpu.VMEM((queries, LANES), F32),
            pltpu.VMEM((queries, features), F32),
            pltpu.VMEM((features, queries), BF16),
            pltpu.VMEM((rows * blocks.shape[0], queries), BF16),
            pltpu.VMEM((2, queries, LANES), F32),
            pltpu.VMEM((queries, LANES), I32),
            pltpu.VMEM((queries, width), BF16),
            pltpu.VMEM((queries, width), BF16),
        ],
        compiler_params=pltpu.CompilerParams(vmem_limit_bytes=(28 if n_t * queries * width * 4 <= 8 * MIB else 60) * MIB),
        cost_estimate=cost(20 * 10**9, 20 * 10**6),
    )(woff, tbase, blocks, frow, pos, wt, *q_pieces, *w_pieces, *groups)


def words_kernel(words, block, grads_ref, *refs):
    code_refs, (out_ref, codes) = refs[:-2], refs[-2:]
    held, sub = out_ref.shape[0], out_ref.shape[1]
    column = 0
    for code_ref in code_refs:
        width = code_ref.shape[3]
        for j in range(code_ref.shape[0]):
            codes[:, column : column + width] = code_ref[j, block]
            column += width
    low = words // SPLIT
    shift = low.bit_length() - 1
    step = 1024

    def body(group, _):
        code8 = codes[pl.ds(pl.multiple_of(8 * group, 8), 8), :]
        for i in range(8):
            m = 8 * group + i
            grad = grads_ref[pl.ds(pl.multiple_of(sub * m, sub), sub), :]
            upper = grad.astype(BF16).astype(F32)
            parts = jnp.concatenate([upper, grad - upper], 0)
            row = code8[i : i + 1, :]
            acc = None
            for t in range(0, codes.shape[1], step):
                c = row[:, t : t + step]
                p = parts[:, t : t + step]
                high = jnp.broadcast_to(lax.shift_right_logical(c, shift), p.shape)
                p = jnp.concatenate([jnp.where(high == h, p, 0.0) for h in range(SPLIT)], 0)
                hot = (c & (low - 1)) == lax.broadcasted_iota(I32, (low, step), 0)
                r = lax.dot_general(
                    hot.astype(F32).astype(BF16), p.astype(BF16), NT, preferred_element_type=F32
                )
                acc = r if acc is None else acc + r
            acc = acc.T
            pieces = []
            for h in range(SPLIT):
                a = acc[2 * sub * h : 2 * sub * h + sub]
                pieces.append(a + acc[2 * sub * h + sub : 2 * sub * (h + 1)])
            out_ref[m] = jnp.concatenate(pieces, 1)
        return 0

    lax.fori_loop(0, held // 8, body, 0)


def word_grads(block, held, words, grads, codes):
    columns = grads.shape[1]
    sub = grads.shape[0] // held
    return pl.pallas_call(
        functools.partial(words_kernel, words, block),
        out_shape=jax.ShapeDtypeStruct((held, sub, words), F32),
        in_specs=[VMEM] * (1 + len(codes)),
        out_specs=VMEM,
        scratch_shapes=[pltpu.VMEM((held, columns), I32)],
        compiler_params=pltpu.CompilerParams(vmem_limit_bytes=8 * MIB),
        cost_estimate=cost(3 * 10**9, 4 * 10**6),
    )(grads, *codes)


def compute(n_dom, n_sh, n_dp, queries_in, encoder_weight, codebook, codes, positive_ids, loss_weight):
    dom, z, x = (lax.axis_index(a) for a in ("dom", "shard", "dp"))
    n_dev = n_dom * n_sh * n_dp
    group = min(n_sh, 4)
    n_zp, zp, zi = n_sh // group, z // group, lax.rem(z, group)
    evens = range(0, n_dom, 2)
    shards = [lax.rem(z - k + n_sh, n_sh) for k in range(n_sh)]
    lanes = [lax.rem(x - t + n_dp, n_dp) for t in range(n_dp)]
    move = lax.ppermute

    w_rows, depth = encoder_weight.shape
    book = codebook[0].astype(BF16)
    words, sub = book.shape[2], book.shape[1]
    held_words = book.shape[0] // n_dp
    columns = depth // words

    def packed(t):
        mine = lax.dynamic_slice_in_dim(book, lanes[t] * held_words, held_words, 0)
        return jnp.concatenate(jnp.split(mine.reshape(held_words * sub, words), columns), 1)

    packs = [packed(t) for t in range(n_dp)]
    packet = jnp.concatenate([encoder_weight, packs[0]])
    moved = [move(packet, "shard", ring(n_sh, k)) for k in range(1, n_sh)]
    w_z = jnp.stack([encoder_weight] + [m[:w_rows] for m in moved])
    moved = jnp.concatenate([m[w_rows:] for m in moved])
    books = [packs[0]] + jnp.split(moved, n_sh - 1)
    for t in range(1, n_dp):
        across = move(moved, "dp", ring(n_dp, t))
        books += [packs[t]] + jnp.split(across, n_sh - 1)
    place = jnp.stack([shards[k] * n_dp + lanes[t] for t in range(n_dp) for k in range(n_sh)]).astype(I32)

    codes_t = codes[0].T.astype(BF16)
    subspaces, pass_rows = codes_t.shape
    width = pass_rows // n_dp
    share = [lax.dynamic_slice_in_dim(codes_t, lanes[t] * width, width, 1) for t in range(n_dp)]
    tiles = {(0, 0): share[0]}
    for k in relay(n_sh):
        step = 1 if 2 * k <= n_sh else n_sh - 1
        source = tiles[0, (k - step) % n_sh]
        tiles[0, k] = move(source, "shard", ring(n_sh, step))
    for t in range(1, n_dp):
        tiles[t, 0] = share[t]
        for k in range(1, n_sh):
            tiles[t, k] = move(tiles[0, k], "dp", ring(n_dp, t))

    q = queries_in[0]
    own = q.shape[0]
    q_held = {0: q}
    for k in relay(group):
        step = 1 if 2 * k <= group else group - 1
        pairs = [(s, s // group * group + (s + step) % group) for s in range(n_sh)]
        q_held[k] = move(q_held[(k - step) % group], "shard", pairs)
    q_pieces = [q_held[k] for k in range(group)]
    q_from = [(zp * group + lax.rem(zi - k + group, group)) * n_dp + x for k in range(group)]

    w_pieces, w_places = [], []
    for e in evens:
        for t in range(n_dp):
            pairs = []
            for d in range(n_dom):
                for c in range(n_dp):
                    pairs.append((d * n_dp + c, (d ^ e) * n_dp + (c + t) % n_dp))
            w_pieces.append(w_z if e == t == 0 else move(w_z, ("dom", "dp"), pairs))
    w_pieces += [move(piece, "dom", flip(n_dom, 1)) for piece in w_pieces]
    for core in range(2):
        for e in evens:
            for t in range(n_dp):
                for k in range(n_sh):
                    w_places.append(((dom ^ (e | core)) * n_sh + shards[k]) * n_dp + lanes[t])
    w_places = jnp.stack(w_places).astype(I32)
    if w_rows % 16:
        whole = jnp.concatenate(w_pieces).reshape(n_dev, w_rows, depth)
        order = jnp.zeros((n_dev,), I32).at[w_places].set(jnp.arange(n_dev, dtype=I32))
        w_pieces = [whole[order].reshape(1, n_dev * w_rows, depth)]
        w_offsets = jnp.zeros((1,), I32)
    else:
        w_offsets = w_places * w_rows

    held = subspaces // (n_sh * n_dp)
    owners = []
    for j in range(n_zp):
        for t in range(n_dp):
            owners.append((lax.rem(zp + j, n_zp) * group + zi) * n_dp + lax.rem(x + t, n_dp))
    blocks = jnp.stack(owners).astype(I32)

    order = [[(t, 0) for t in range(n_dp)]] + [[(t, k) for k in range(1, n_sh)] for t in range(n_dp)]
    bases = [shards[k] * pass_rows + lanes[t] * width for part in order for t, k in part]
    built = []
    for part in order:
        built.append(rebuild(place, blocks, held, sub, words, [tiles[key] for key in part], books))
    passages = [b[0] for b in built]
    tile_codes = [b[1] for b in built]

    def rows_of(array):
        return jnp.concatenate([lax.dynamic_slice_in_dim(array, f * own, own, 0) for f in q_from])[:, None]

    out_rows = depth // n_dev
    firsts = []
    for core in range(2):
        for e in evens:
            for owner in owners:
                firsts.append(((dom ^ (e | core)) * n_sh * n_dp + owner) * out_rows)
    frow = (jnp.stack(firsts).astype(I32)[:, None] + jnp.arange(out_rows, dtype=I32)[None, :]).reshape(-1, 1)

    own_part, other_part, *grads = main(
        w_offsets,
        jnp.stack(bases).astype(I32),
        blocks,
        held * (depth // subspaces),
        frow,
        rows_of(positive_ids[0]),
        rows_of(loss_weight[0].astype(F32)),
        q_pieces,
        w_pieces,
        passages,
    )

    summed = own_part + move(other_part, "dom", flip(n_dom, 1))
    summed = summed.reshape(len(evens), len(owners), out_rows, depth)
    weight_grad = summed[0, 0]
    book_grad = None
    for o in reversed(range(len(owners))):
        j, t = o // n_dp, o % n_dp
        part = word_grads(o, held, words, grads[o], tile_codes)
        if o:
            pairs = []
            for s in range(n_sh):
                for d in range(n_dp):
                    pairs.append((s * n_dp + d, (s + group * j) % n_sh * n_dp + (d + t) % n_dp))
            part = move(part, ("shard", "dp"), pairs)
        book_grad = part if book_grad is None else book_grad + part
    for i, e in enumerate(evens):
        for o in range(len(owners)):
            if i == o == 0:
                continue
            j, t = o // n_dp, o % n_dp
            pairs = []
            for d in range(n_dom):
                for s in range(n_sh):
                    for c in range(n_dp):
                        to = ((d ^ e) * n_sh + (s + group * j) % n_sh) * n_dp + (c + t) % n_dp
                        pairs.append(((d * n_sh + s) * n_dp + c, to))
            moved = move(summed[i, o], ("dom", "shard", "dp"), pairs)
            weight_grad = weight_grad + moved
    return (weight_grad, book_grad[None])


def solution(mesh):
    sizes = [mesh.shape[a] for a in ("dom", "shard", "dp")]
    return jax.shard_map(
        functools.partial(compute, *sizes),
        mesh=mesh,
        in_specs=(
            P("dom", ("shard", "dp"), None),
            P(("dom", "shard", "dp"), None),
            P("dom", "shard", None, None),
            P("dom", "shard", None),
            P("dom", None),
            P("dom", None),
        ),
        out_specs=(P(("dom", "shard", "dp"), None), P("dom", ("shard", "dp"), None, None)),
        check_vma=False,
    )
```

```python
import functools
import jax
import jax.numpy as jnp
from jax import lax
from jax.experimental import pallas as pl
from jax.experimental.pallas import tpu as pltpu
from jax.sharding import PartitionSpec as P


BF16, F32, I32 = jnp.bfloat16, jnp.float32, jnp.int32
NT = (((1,), (1,)), ((), ()))
LANES = 128
SPLIT = 4
ANY = pl.BlockSpec(memory_space=pl.ANY)
VMEM = pl.BlockSpec(memory_space=pltpu.VMEM)
SMEM = pl.BlockSpec(memory_space=pltpu.SMEM)
SPAN = 64
MIB = 2**20


def ring(n, k):
    return [(i, (i + k) % n) for i in range(n)]


def flip(n, k):
    return [(i, i ^ k) for i in range(n)]


def relay(n):
    return list(range(1, n // 2 + 1)) + list(range(n - 1, n // 2, -1))


def cost(flops, bytes_accessed):
    return pl.CostEstimate(flops=flops, bytes_accessed=bytes_accessed, transcendentals=0)


def rebuild_kernel(n_t, n_b, place_ref, blocks_ref, *refs):
    code_refs, books = refs[:n_t], refs[n_t : n_t + n_b]
    out_ref, kept_ref, codes_ref, *tables = refs[n_t + n_b :]
    columns = code_refs[0].shape[1]
    kept = kept_ref.shape[2]
    words = len(tables) * LANES
    for i, code_ref in enumerate(code_refs):
        codes_ref[i] = code_ref[...].astype(I32)
        for b in range(kept_ref.shape[1]):
            kept_ref[i, b] = codes_ref[i, pl.ds(pl.multiple_of(blocks_ref[b] * kept, kept), kept), :]
    for piece, book_ref in enumerate(books):
        rows = book_ref.shape[0]
        blocks = book_ref.shape[1] // words
        for c in range(blocks):
            at = pl.ds(pl.multiple_of((place_ref[piece] * blocks + c) * rows, rows), rows)
            for i, table in enumerate(tables):
                first = c * words + i * LANES
                table[at, :] = book_ref[:, first : first + LANES].astype(F32)
    subspaces = code_refs[0].shape[0]
    span = min(subspaces, SPAN)
    steps = subspaces // span
    sub = tables[0].shape[0] // subspaces

    def body(i, _):
        tile, first = i // steps, lax.rem(i, steps) * span
        for j in range(span // 8):
            rows = pl.multiple_of(first + 8 * j, 8)
            index = codes_ref[tile, pl.ds(rows, 8), :]
            for pair in range(0, sub, 2):
                held = []
                for f in range(pair, pair + 2):
                    held.append([table[pl.ds(rows * sub + f, 8, stride=sub), :] for table in tables])
                for t in range(0, columns, LANES):
                    code = index[:, t : t + LANES]
                    lane = code & (LANES - 1)
                    parts = []
                    for f in range(2):
                        value = None
                        for c, part in enumerate(held[f]):
                            found = jnp.take_along_axis(part, lane, axis=1, mode="promise_in_bounds")
                            value = found if value is None else jnp.where(code < c * LANES, value, found)
                        parts.append(value)
                    out_rows = pl.ds(pl.multiple_of(rows * sub + 8 * pair, 16), 16)
                    out_ref[tile, out_rows, t : t + LANES] = jnp.concatenate(parts, 0).astype(BF16)
        return 0

    lax.fori_loop(0, n_t * steps, body, 0)


def regroup(x):
    lane = lax.broadcasted_iota(I32, (x.shape[0], LANES), 1)
    lane = (lane & 64) + (lane & 7) * 8 + (lax.shift_right_logical(lane, 3) & 7)
    parts = [x[:, c : c + LANES] for c in range(0, x.shape[1], LANES)]
    return jnp.concatenate(
        [jnp.take_along_axis(p, lane, axis=1, mode="promise_in_bounds") for p in parts], 1
    )


def rebuild(place, blocks, kept, sub, words, codes, books):
    n_t, n_b = len(codes), len(books)
    subspaces, columns = codes[0].shape
    return pl.pallas_call(
        functools.partial(rebuild_kernel, n_t, n_b),
        out_shape=(
            jax.ShapeDtypeStruct((n_t, subspaces * sub, columns), BF16),
            jax.ShapeDtypeStruct((n_t, blocks.shape[0], kept, columns), I32),
        ),
        in_specs=[SMEM, SMEM] + [VMEM] * (n_t + n_b),
        out_specs=(VMEM, VMEM),
        scratch_shapes=[
            pltpu.VMEM((n_t, subspaces, columns), I32),
        ]
        + [pltpu.VMEM((subspaces * sub, LANES), F32)] * (words // LANES),
        compiler_params=pltpu.CompilerParams(vmem_limit_bytes=(6 + n_t) * MIB),
        cost_estimate=cost(n_t * 10**9, n_t * 2 * 10**6),
    )(place, blocks, *codes, *books)


def main_kernel(n_q, n_w, n_g, woff_ref, tbase_ref, blocks_ref, frow_ref, pos_ref, wt_ref, *refs):
    q_refs, refs = refs[:n_q], refs[n_q:]
    w_refs, refs = refs[:n_w], refs[n_w:]
    g_refs, refs = refs[:n_g], refs[n_g:]
    own_ref, other_ref, grads_refs, refs = refs[0], refs[1], refs[2:-12], refs[-12:]
    w, q, exps, normed, total, gn, nt, some, ahead, places, even, odd = refs
    for i, w_ref in enumerate(w_refs):
        blocks, rows = w_ref.shape[0], w_ref.shape[1]
        for k in range(blocks):
            w[pl.ds(pl.multiple_of(woff_ref[i * blocks + k], rows), rows), :] = w_ref[k]
    own = q_refs[0].shape[0]
    for i, q_ref in enumerate(q_refs):
        q[i * own : (i + 1) * own, :] = q_ref[...]
    depth = q.shape[1]
    rows = frow_ref.shape[0]
    pick = (frow_ref[...] == lax.broadcasted_iota(I32, (rows, depth), 1)).astype(F32).astype(BF16)
    picked = lax.dot_general(pick, q[...], NT, preferred_element_type=F32).astype(BF16)
    encoded = jnp.dot(q[...], w[...], preferred_element_type=F32)
    inv_rms = lax.rsqrt(jnp.mean(encoded * encoded, axis=1, keepdims=True) + 1e-06)
    normed[...] = encoded * inv_rms
    low = normed[...].astype(BF16)
    q[...] = regroup(normed[...]).astype(BF16)
    nt[...] = low.T
    features = grads_refs[0].shape[0]
    for i in range(len(grads_refs)):
        at = pl.ds(pl.multiple_of(blocks_ref[i] * features, features), features)
        some[i * features : (i + 1) * features, :] = nt[at, :]
    at = [(tiles, j) for tiles in g_refs for j in range(tiles.shape[0])]
    width = at[0][0].shape[2]
    spread = [pl.ds(c, LANES) for c in range(0, width, LANES)]
    total[...] = jnp.zeros_like(total)

    def exponent(n):
        part = total[...]
        for c in spread:
            e = jnp.exp(exps[n, :, c])
            exps[n, :, c] = e
            part = part + e
        total[...] = part

    for n, (tiles, j) in enumerate(at):
        exps[n] = jnp.dot(q[...], tiles[j], preferred_element_type=F32)
        if n:
            exponent(n - 1)
    exponent(len(at) - 1)
    scale = wt_ref[...] / jnp.sum(total[...], axis=1, keepdims=True)
    ahead[0] = jnp.broadcast_to(scale, total.shape)
    ahead[1] = jnp.broadcast_to(wt_ref[...], total.shape)
    places[...] = jnp.broadcast_to(pos_ref[...], total.shape)
    lane = lax.broadcasted_iota(I32, (1, LANES), 1)

    def weigh(n):
        out = (even, odd)[n % 2]
        for i, c in enumerate(spread):
            hit = places[...] == lane + (tbase_ref[n] + i * LANES)
            out[:, c] = (exps[n, :, c] * ahead[0] - jnp.where(hit, ahead[1], 0.0)).astype(BF16)

    weigh(0)
    for n, (tiles, j) in enumerate(at):
        gs = (even, odd)[n % 2]
        if n + 1 < len(at):
            weigh(n + 1)
        more = lax.dot_general(gs[...], tiles[j], NT, preferred_element_type=F32)
        gn[...] = more if n == 0 else gn[...] + more
        grads = jnp.dot(some[...], gs[...], preferred_element_type=F32)
        for i, grads_ref in enumerate(grads_refs):
            grads_ref[:, n * width : (n + 1) * width] = grads[i * features : (i + 1) * features]
    gn[...] = regroup(gn[...])
    inner = jnp.mean(gn[...] * normed[...], axis=1, keepdims=True)
    grad = (inv_rms * (gn[...] - normed[...] * inner)).astype(BF16)
    half = rows // 2
    own_ref[...] = jnp.dot(picked[:half], grad, preferred_element_type=F32)
    other_ref[...] = jnp.dot(picked[half:], grad, preferred_element_type=F32)


def main(woff, tbase, blocks, rows, frow, pos, wt, q_pieces, w_pieces, groups):
    n_q, n_w, n_g = len(q_pieces), len(w_pieces), len(groups)
    own, depth = q_pieces[0].shape
    queries = own * n_q
    n_t = sum(g.shape[0] for g in groups)
    features, width = groups[0].shape[1:]
    half = frow.shape[0] // 2
    return pl.pallas_call(
        functools.partial(main_kernel, n_q, n_w, n_g),
        out_shape=(jax.ShapeDtypeStruct((half, features), F32),) * 2
        + (jax.ShapeDtypeStruct((rows, n_t * width), F32),) * blocks.shape[0],
        in_specs=[SMEM, SMEM, SMEM, VMEM, VMEM, VMEM] + [VMEM] * (n_q + n_w + n_g),
        out_specs=(VMEM,) * (2 + blocks.shape[0]),
        scratch_shapes=[
            pltpu.VMEM((depth, features), BF16),
            pltpu.VMEM((queries, depth), BF16),
            pltpu.VMEM((n_t, queries, width), F32),
            pltpu.VMEM((queries, features), F32),
            pltpu.VMEM((queries, LANES), F32),
            pltpu.VMEM((queries, features), F32),
            pltpu.VMEM((features, queries), BF16),
            pltpu.VMEM((rows * blocks.shape[0], queries), BF16),
            pltpu.VMEM((2, queries, LANES), F32),
            pltpu.VMEM((queries, LANES), I32),
            pltpu.VMEM((queries, width), BF16),
            pltpu.VMEM((queries, width), BF16),
        ],
        compiler_params=pltpu.CompilerParams(vmem_limit_bytes=(28 if n_t * queries * width * 4 <= 8 * MIB else 60) * MIB),
        cost_estimate=cost(20 * 10**9, 20 * 10**6),
    )(woff, tbase, blocks, frow, pos, wt, *q_pieces, *w_pieces, *groups)


def words_kernel(words, block, grads_ref, *refs):
    code_refs, (out_ref, codes) = refs[:-2], refs[-2:]
    held, sub = out_ref.shape[0], out_ref.shape[1]
    column = 0
    for code_ref in code_refs:
        width = code_ref.shape[3]
        for j in range(code_ref.shape[0]):
            codes[:, column : column + width] = code_ref[j, block]
            column += width
    low = words // SPLIT
    shift = low.bit_length() - 1
    step = 1024

    def body(group, _):
        code8 = codes[pl.ds(pl.multiple_of(8 * group, 8), 8), :]
        for i in range(8):
            m = 8 * group + i
            grad = grads_ref[pl.ds(pl.multiple_of(sub * m, sub), sub), :]
            upper = grad.astype(BF16).astype(F32)
            parts = jnp.concatenate([upper, grad - upper], 0)
            row = code8[i : i + 1, :]
            acc = None
            for t in range(0, codes.shape[1], step):
                c = row[:, t : t + step]
                p = parts[:, t : t + step]
                high = jnp.broadcast_to(lax.shift_right_logical(c, shift), p.shape)
                p = jnp.concatenate([jnp.where(high == h, p, 0.0) for h in range(SPLIT)], 0)
                hot = (c & (low - 1)) == lax.broadcasted_iota(I32, (low, step), 0)
                r = lax.dot_general(
                    hot.astype(F32).astype(BF16), p.astype(BF16), NT, preferred_element_type=F32
                )
                acc = r if acc is None else acc + r
            acc = acc.T
            pieces = []
            for h in range(SPLIT):
                a = acc[2 * sub * h : 2 * sub * h + sub]
                pieces.append(a + acc[2 * sub * h + sub : 2 * sub * (h + 1)])
            out_ref[m] = jnp.concatenate(pieces, 1)
        return 0

    lax.fori_loop(0, held // 8, body, 0)


def word_grads(block, held, words, grads, codes):
    columns = grads.shape[1]
    sub = grads.shape[0] // held
    return pl.pallas_call(
        functools.partial(words_kernel, words, block),
        out_shape=jax.ShapeDtypeStruct((held, sub, words), F32),
        in_specs=[VMEM] * (1 + len(codes)),
        out_specs=VMEM,
        scratch_shapes=[pltpu.VMEM((held, columns), I32)],
        compiler_params=pltpu.CompilerParams(vmem_limit_bytes=8 * MIB),
        cost_estimate=cost(3 * 10**9, 4 * 10**6),
    )(grads, *codes)


def compute(n_dom, n_sh, n_dp, queries_in, encoder_weight, codebook, codes, positive_ids, loss_weight):
    dom, z, x = (lax.axis_index(a) for a in ("dom", "shard", "dp"))
    n_dev = n_dom * n_sh * n_dp
    group = min(n_sh, 4)
    n_zp, zp, zi = n_sh // group, z // group, lax.rem(z, group)
    evens = range(0, n_dom, 2)
    shards = [lax.rem(z - k + n_sh, n_sh) for k in range(n_sh)]
    lanes = [lax.rem(x - t + n_dp, n_dp) for t in range(n_dp)]
    move = lax.ppermute

    w_rows, depth = encoder_weight.shape
    book = codebook[0].astype(BF16)
    words, sub = book.shape[2], book.shape[1]
    held_words = book.shape[0] // n_dp
    columns = depth // words

    def packed(t):
        mine = lax.dynamic_slice_in_dim(book, lanes[t] * held_words, held_words, 0)
        return jnp.concatenate(jnp.split(mine.reshape(held_words * sub, words), columns), 1)

    packs = [packed(t) for t in range(n_dp)]
    packet = jnp.concatenate([encoder_weight, packs[0]])
    moved = [move(packet, "shard", ring(n_sh, k)) for k in range(1, n_sh)]
    w_z = jnp.stack([encoder_weight] + [m[:w_rows] for m in moved])
    moved = jnp.concatenate([m[w_rows:] for m in moved])
    books = [packs[0]] + jnp.split(moved, n_sh - 1)
    for t in range(1, n_dp):
        across = move(moved, "dp", ring(n_dp, t))
        books += [packs[t]] + jnp.split(across, n_sh - 1)
    place = jnp.stack([shards[k] * n_dp + lanes[t] for t in range(n_dp) for k in range(n_sh)]).astype(I32)

    codes_t = codes[0].T.astype(BF16)
    subspaces, pass_rows = codes_t.shape
    width = pass_rows // n_dp
    share = [lax.dynamic_slice_in_dim(codes_t, lanes[t] * width, width, 1) for t in range(n_dp)]
    tiles = {(0, 0): share[0]}
    for k in relay(n_sh):
        step = 1 if 2 * k <= n_sh else n_sh - 1
        source = tiles[0, (k - step) % n_sh]
        tiles[0, k] = move(source, "shard", ring(n_sh, step))
    for t in range(1, n_dp):
        tiles[t, 0] = share[t]
        for k in range(1, n_sh):
            tiles[t, k] = move(tiles[0, k], "dp", ring(n_dp, t))

    q = queries_in[0]
    own = q.shape[0]
    q_held = {0: q}
    for k in relay(group):
        step = 1 if 2 * k <= group else group - 1
        pairs = [(s, s // group * group + (s + step) % group) for s in range(n_sh)]
        q_held[k] = move(q_held[(k - step) % group], "shard", pairs)
    q_pieces = [q_held[k] for k in range(group)]
    q_from = [(zp * group + lax.rem(zi - k + group, group)) * n_dp + x for k in range(group)]

    w_pieces, w_places = [], []
    for e in evens:
        for t in range(n_dp):
            pairs = []
            for d in range(n_dom):
                for c in range(n_dp):
                    pairs.append((d * n_dp + c, (d ^ e) * n_dp + (c + t) % n_dp))
            w_pieces.append(w_z if e == t == 0 else move(w_z, ("dom", "dp"), pairs))
    w_pieces += [move(piece, "dom", flip(n_dom, 1)) for piece in w_pieces]
    for core in range(2):
        for e in evens:
            for t in range(n_dp):
                for k in range(n_sh):
                    w_places.append(((dom ^ (e | core)) * n_sh + shards[k]) * n_dp + lanes[t])
    w_places = jnp.stack(w_places).astype(I32)
    if w_rows % 16:
        whole = jnp.concatenate(w_pieces).reshape(n_dev, w_rows, depth)
        order = jnp.zeros((n_dev,), I32).at[w_places].set(jnp.arange(n_dev, dtype=I32))
        w_pieces = [whole[order].reshape(1, n_dev * w_rows, depth)]
        w_offsets = jnp.zeros((1,), I32)
    else:
        w_offsets = w_places * w_rows

    held = subspaces // (n_sh * n_dp)
    owners = []
    for j in range(n_zp):
        for t in range(n_dp):
            owners.append((lax.rem(zp + j, n_zp) * group + zi) * n_dp + lax.rem(x + t, n_dp))
    blocks = jnp.stack(owners).astype(I32)

    order = [[(t, 0) for t in range(n_dp)]] + [[(t, k) for k in range(1, n_sh)] for t in range(n_dp)]
    bases = [shards[k] * pass_rows + lanes[t] * width for part in order for t, k in part]
    built = []
    for part in order:
        built.append(rebuild(place, blocks, held, sub, words, [tiles[key] for key in part], books))
    passages = [b[0] for b in built]
    tile_codes = [b[1] for b in built]

    def rows_of(array):
        return jnp.concatenate([lax.dynamic_slice_in_dim(array, f * own, own, 0) for f in q_from])[:, None]

    out_rows = depth // n_dev
    firsts = []
    for core in range(2):
        for e in evens:
            for owner in owners:
                firsts.append(((dom ^ (e | core)) * n_sh * n_dp + owner) * out_rows)
    frow = (jnp.stack(firsts).astype(I32)[:, None] + jnp.arange(out_rows, dtype=I32)[None, :]).reshape(-1, 1)

    own_part, other_part, *grads = main(
        w_offsets,
        jnp.stack(bases).astype(I32),
        blocks,
        held * (depth // subspaces),
        frow,
        rows_of(positive_ids[0]),
        rows_of(loss_weight[0].astype(F32)),
        q_pieces,
        w_pieces,
        passages,
    )

    summed = own_part + move(other_part, "dom", flip(n_dom, 1))
    summed = summed.reshape(len(evens), len(owners), out_rows, depth)
    weight_grad = summed[0, 0]
    book_grad = None
    for o in reversed(range(len(owners))):
        j, t = o // n_dp, o % n_dp
        part = word_grads(o, held, words, grads[o], tile_codes)
        if o:
            pairs = []
            for s in range(n_sh):
                for d in range(n_dp):
                    pairs.append((s * n_dp + d, (s + group * j) % n_sh * n_dp + (d + t) % n_dp))
            part = move(part, ("shard", "dp"), pairs)
        book_grad = part if book_grad is None else book_grad + part
    for i, e in enumerate(evens):
        for o in range(len(owners)):
            if i == o == 0:
                continue
            j, t = o // n_dp, o % n_dp
            pairs = []
            for d in range(n_dom):
                for s in range(n_sh):
                    for c in range(n_dp):
                        to = ((d ^ e) * n_sh + (s + group * j) % n_sh) * n_dp + (c + t) % n_dp
                        pairs.append(((d * n_sh + s) * n_dp + c, to))
            moved = move(summed[i, o], ("dom", "shard", "dp"), pairs)
            weight_grad = weight_grad + moved
    return (weight_grad, book_grad[None])


def solution(mesh):
    sizes = [mesh.shape[a] for a in ("dom", "shard", "dp")]
    return jax.shard_map(
        functools.partial(compute, *sizes),
        mesh=mesh,
        in_specs=(
            P("dom", ("shard", "dp"), None),
            P(("dom", "shard", "dp"), None),
            P("dom", "shard", None, None),
            P("dom", "shard", None),
            P("dom", None),
            P("dom", None),
        ),
        out_specs=(P(("dom", "shard", "dp"), None), P("dom", ("shard", "dp"), None, None)),
        check_vma=False,
    )
```

```python
import functools
import jax
import jax.numpy as jnp
from jax import lax
from jax.experimental import pallas as pl
from jax.experimental.pallas import tpu as pltpu
from jax.sharding import PartitionSpec as P


BF16, F32, I32 = jnp.bfloat16, jnp.float32, jnp.int32
NT = (((1,), (1,)), ((), ()))
LANES = 128
SPLIT = 4
ANY = pl.BlockSpec(memory_space=pl.ANY)
VMEM = pl.BlockSpec(memory_space=pltpu.VMEM)
SMEM = pl.BlockSpec(memory_space=pltpu.SMEM)
SPAN = 64
MIB = 2**20


def ring(n, k):
    return [(i, (i + k) % n) for i in range(n)]


def flip(n, k):
    return [(i, i ^ k) for i in range(n)]


def relay(n):
    return list(range(1, n // 2 + 1)) + list(range(n - 1, n // 2, -1))


def cost(flops, bytes_accessed):
    return pl.CostEstimate(flops=flops, bytes_accessed=bytes_accessed, transcendentals=0)


def rebuild_kernel(n_t, n_b, place_ref, blocks_ref, *refs):
    code_refs, books = refs[:n_t], refs[n_t : n_t + n_b]
    out_ref, kept_ref, codes_ref, table = refs[n_t + n_b :]
    sub, words = table.shape[1:]
    columns = code_refs[0].shape[1]
    kept = kept_ref.shape[2]
    for i, code_ref in enumerate(code_refs):
        codes_ref[i] = code_ref[...].astype(I32)
        for b in range(kept_ref.shape[1]):
            kept_ref[i, b] = codes_ref[i, pl.ds(pl.multiple_of(blocks_ref[b] * kept, kept), kept), :]
    for piece, book_ref in enumerate(books):
        some = book_ref.shape[0] // sub
        blocks = book_ref.shape[1] // words
        for c in range(blocks):
            part = book_ref[:, c * words : (c + 1) * words].astype(F32).reshape(some, sub, words)
            table[pl.ds((place_ref[piece] * blocks + c) * some, some)] = part

    subspaces = code_refs[0].shape[0]
    span = min(subspaces, SPAN)
    steps = subspaces // span

    def body(i, _):
        tile, first = i // steps, lax.rem(i, steps) * span
        for j in range(span // 8):
            rows = pl.multiple_of(first + 8 * j, 8)
            codes = codes_ref[tile, pl.ds(rows, 8), :]
            for pair in range(4):
                tables = []
                for h in range(2):
                    words_of = table[rows + 2 * pair + h]
                    tables.append([words_of[:, c : c + LANES] for c in range(0, words, LANES)])
                for t in range(0, columns, LANES):
                    parts = []
                    for h in range(2):
                        row = codes[2 * pair + h : 2 * pair + h + 1, t : t + LANES]
                        index = jnp.broadcast_to(row, (sub, LANES))
                        lane = index & (LANES - 1)
                        value = None
                        for c, part in enumerate(tables[h]):
                            found = jnp.take_along_axis(part, lane, axis=1, mode="promise_in_bounds")
                            value = found if value is None else jnp.where(index < c * LANES, value, found)
                        parts.append(value)
                    out_rows = pl.ds(pl.multiple_of((rows + 2 * pair) * sub, 2 * sub), 2 * sub)
                    out_ref[tile, out_rows, t : t + LANES] = jnp.concatenate(parts, 0).astype(BF16)
        return 0

    lax.fori_loop(0, n_t * steps, body, 0)


def rebuild(place, blocks, kept, sub, words, codes, books):
    n_t, n_b = len(codes), len(books)
    subspaces, columns = codes[0].shape
    return pl.pallas_call(
        functools.partial(rebuild_kernel, n_t, n_b),
        out_shape=(
            jax.ShapeDtypeStruct((n_t, subspaces * sub, columns), BF16),
            jax.ShapeDtypeStruct((n_t, blocks.shape[0], kept, columns), I32),
        ),
        in_specs=[SMEM, SMEM] + [VMEM] * (n_t + n_b),
        out_specs=(VMEM, VMEM),
        scratch_shapes=[
            pltpu.VMEM((n_t, subspaces, columns), I32),
            pltpu.VMEM((subspaces, sub, words), F32),
        ],
        compiler_params=pltpu.CompilerParams(vmem_limit_bytes=(6 + n_t) * MIB),
        cost_estimate=cost(n_t * 10**9, n_t * 2 * 10**6),
    )(place, blocks, *codes, *books)


def main_kernel(n_q, n_w, n_g, woff_ref, tbase_ref, blocks_ref, frow_ref, pos_ref, wt_ref, *refs):
    q_refs, refs = refs[:n_q], refs[n_q:]
    w_refs, refs = refs[:n_w], refs[n_w:]
    g_refs, refs = refs[:n_g], refs[n_g:]
    own_ref, other_ref, grads_refs, refs = refs[0], refs[1], refs[2:-12], refs[-12:]
    w, q, exps, normed, total, gn, nt, some, ahead, places, even, odd = refs
    for i, w_ref in enumerate(w_refs):
        blocks, rows = w_ref.shape[0], w_ref.shape[1]
        for k in range(blocks):
            w[pl.ds(pl.multiple_of(woff_ref[i * blocks + k], rows), rows), :] = w_ref[k]
    own = q_refs[0].shape[0]
    for i, q_ref in enumerate(q_refs):
        q[i * own : (i + 1) * own, :] = q_ref[...]
    depth = q.shape[1]
    rows = frow_ref.shape[0]
    pick = (frow_ref[...] == lax.broadcasted_iota(I32, (rows, depth), 1)).astype(F32).astype(BF16)
    picked = lax.dot_general(pick, q[...], NT, preferred_element_type=F32).astype(BF16)
    encoded = jnp.dot(q[...], w[...], preferred_element_type=F32)
    inv_rms = lax.rsqrt(jnp.mean(encoded * encoded, axis=1, keepdims=True) + 1e-06)
    normed[...] = encoded * inv_rms
    low = normed[...].astype(BF16)
    q[...] = low
    nt[...] = low.T
    features = grads_refs[0].shape[0]
    for i in range(len(grads_refs)):
        at = pl.ds(pl.multiple_of(blocks_ref[i] * features, features), features)
        some[i * features : (i + 1) * features, :] = nt[at, :]
    at = [(tiles, j) for tiles in g_refs for j in range(tiles.shape[0])]
    width = at[0][0].shape[2]
    spread = [pl.ds(c, LANES) for c in range(0, width, LANES)]
    total[...] = jnp.zeros_like(total)

    def exponent(n):
        part = total[...]
        for c in spread:
            e = jnp.exp(exps[n, :, c])
            exps[n, :, c] = e
            part = part + e
        total[...] = part

    for n, (tiles, j) in enumerate(at):
        exps[n] = jnp.dot(q[...], tiles[j], preferred_element_type=F32)
        if n:
            exponent(n - 1)
    exponent(len(at) - 1)
    scale = wt_ref[...] / jnp.sum(total[...], axis=1, keepdims=True)
    ahead[0] = jnp.broadcast_to(scale, total.shape)
    ahead[1] = jnp.broadcast_to(wt_ref[...], total.shape)
    places[...] = jnp.broadcast_to(pos_ref[...], total.shape)
    lane = lax.broadcasted_iota(I32, (1, LANES), 1)

    def weigh(n):
        out = (even, odd)[n % 2]
        for i, c in enumerate(spread):
            hit = places[...] == lane + (tbase_ref[n] + i * LANES)
            out[:, c] = (exps[n, :, c] * ahead[0] - jnp.where(hit, ahead[1], 0.0)).astype(BF16)

    weigh(0)
    for n, (tiles, j) in enumerate(at):
        gs = (even, odd)[n % 2]
        if n + 1 < len(at):
            weigh(n + 1)
        more = lax.dot_general(gs[...], tiles[j], NT, preferred_element_type=F32)
        gn[...] = more if n == 0 else gn[...] + more
        grads = jnp.dot(some[...], gs[...], preferred_element_type=F32)
        for i, grads_ref in enumerate(grads_refs):
            grads_ref[:, n * width : (n + 1) * width] = grads[i * features : (i + 1) * features]
    inner = jnp.mean(gn[...] * normed[...], axis=1, keepdims=True)
    grad = (inv_rms * (gn[...] - normed[...] * inner)).astype(BF16)
    half = rows // 2
    own_ref[...] = jnp.dot(picked[:half], grad, preferred_element_type=F32)
    other_ref[...] = jnp.dot(picked[half:], grad, preferred_element_type=F32)


def main(woff, tbase, blocks, rows, frow, pos, wt, q_pieces, w_pieces, groups):
    n_q, n_w, n_g = len(q_pieces), len(w_pieces), len(groups)
    own, depth = q_pieces[0].shape
    queries = own * n_q
    n_t = sum(g.shape[0] for g in groups)
    features, width = groups[0].shape[1:]
    half = frow.shape[0] // 2
    return pl.pallas_call(
        functools.partial(main_kernel, n_q, n_w, n_g),
        out_shape=(jax.ShapeDtypeStruct((half, features), F32),) * 2
        + (jax.ShapeDtypeStruct((rows, n_t * width), F32),) * blocks.shape[0],
        in_specs=[SMEM, SMEM, SMEM, VMEM, VMEM, VMEM] + [VMEM] * (n_q + n_w + n_g),
        out_specs=(VMEM,) * (2 + blocks.shape[0]),
        scratch_shapes=[
            pltpu.VMEM((depth, features), BF16),
            pltpu.VMEM((queries, depth), BF16),
            pltpu.VMEM((n_t, queries, width), F32),
            pltpu.VMEM((queries, features), F32),
            pltpu.VMEM((queries, LANES), F32),
            pltpu.VMEM((queries, features), F32),
            pltpu.VMEM((features, queries), BF16),
            pltpu.VMEM((rows * blocks.shape[0], queries), BF16),
            pltpu.VMEM((2, queries, LANES), F32),
            pltpu.VMEM((queries, LANES), I32),
            pltpu.VMEM((queries, width), BF16),
            pltpu.VMEM((queries, width), BF16),
        ],
        compiler_params=pltpu.CompilerParams(vmem_limit_bytes=(28 if n_t * queries * width * 4 <= 8 * MIB else 60) * MIB),
        cost_estimate=cost(20 * 10**9, 20 * 10**6),
    )(woff, tbase, blocks, frow, pos, wt, *q_pieces, *w_pieces, *groups)


def words_kernel(words, block, grads_ref, *refs):
    code_refs, (out_ref, codes) = refs[:-2], refs[-2:]
    held, sub = out_ref.shape[0], out_ref.shape[1]
    column = 0
    for code_ref in code_refs:
        width = code_ref.shape[3]
        for j in range(code_ref.shape[0]):
            codes[:, column : column + width] = code_ref[j, block]
            column += width
    low = words // SPLIT
    shift = low.bit_length() - 1
    step = 1024

    def body(group, _):
        code8 = codes[pl.ds(pl.multiple_of(8 * group, 8), 8), :]
        for i in range(8):
            m = 8 * group + i
            grad = grads_ref[pl.ds(pl.multiple_of(sub * m, sub), sub), :]
            upper = grad.astype(BF16).astype(F32)
            parts = jnp.concatenate([upper, grad - upper], 0)
            row = code8[i : i + 1, :]
            acc = None
            for t in range(0, codes.shape[1], step):
                c = row[:, t : t + step]
                p = parts[:, t : t + step]
                high = jnp.broadcast_to(lax.shift_right_logical(c, shift), p.shape)
                p = jnp.concatenate([jnp.where(high == h, p, 0.0) for h in range(SPLIT)], 0)
                hot = (c & (low - 1)) == lax.broadcasted_iota(I32, (low, step), 0)
                r = lax.dot_general(
                    hot.astype(F32).astype(BF16), p.astype(BF16), NT, preferred_element_type=F32
                )
                acc = r if acc is None else acc + r
            acc = acc.T
            pieces = []
            for h in range(SPLIT):
                a = acc[2 * sub * h : 2 * sub * h + sub]
                pieces.append(a + acc[2 * sub * h + sub : 2 * sub * (h + 1)])
            out_ref[m] = jnp.concatenate(pieces, 1)
        return 0

    lax.fori_loop(0, held // 8, body, 0)


def word_grads(block, held, words, grads, codes):
    columns = grads.shape[1]
    sub = grads.shape[0] // held
    return pl.pallas_call(
        functools.partial(words_kernel, words, block),
        out_shape=jax.ShapeDtypeStruct((held, sub, words), F32),
        in_specs=[VMEM] * (1 + len(codes)),
        out_specs=VMEM,
        scratch_shapes=[pltpu.VMEM((held, columns), I32)],
        compiler_params=pltpu.CompilerParams(vmem_limit_bytes=8 * MIB),
        cost_estimate=cost(3 * 10**9, 4 * 10**6),
    )(grads, *codes)


def compute(n_dom, n_sh, n_dp, queries_in, encoder_weight, codebook, codes, positive_ids, loss_weight):
    dom, z, x = (lax.axis_index(a) for a in ("dom", "shard", "dp"))
    n_dev = n_dom * n_sh * n_dp
    group = min(n_sh, 4)
    n_zp, zp, zi = n_sh // group, z // group, lax.rem(z, group)
    evens = range(0, n_dom, 2)
    shards = [lax.rem(z - k + n_sh, n_sh) for k in range(n_sh)]
    lanes = [lax.rem(x - t + n_dp, n_dp) for t in range(n_dp)]
    move = lax.ppermute

    w_rows, depth = encoder_weight.shape
    book = codebook[0].astype(BF16)
    words, sub = book.shape[2], book.shape[1]
    held_words = book.shape[0] // n_dp
    columns = depth // words

    def packed(t):
        mine = lax.dynamic_slice_in_dim(book, lanes[t] * held_words, held_words, 0)
        return jnp.concatenate(jnp.split(mine.reshape(held_words * sub, words), columns), 1)

    packs = [packed(t) for t in range(n_dp)]
    packet = jnp.concatenate([encoder_weight, packs[0]])
    moved = [move(packet, "shard", ring(n_sh, k)) for k in range(1, n_sh)]
    w_z = jnp.stack([encoder_weight] + [m[:w_rows] for m in moved])
    moved = jnp.concatenate([m[w_rows:] for m in moved])
    books = [packs[0]] + jnp.split(moved, n_sh - 1)
    for t in range(1, n_dp):
        across = move(moved, "dp", ring(n_dp, t))
        books += [packs[t]] + jnp.split(across, n_sh - 1)
    place = jnp.stack([shards[k] * n_dp + lanes[t] for t in range(n_dp) for k in range(n_sh)]).astype(I32)

    codes_t = codes[0].T.astype(BF16)
    subspaces, pass_rows = codes_t.shape
    width = pass_rows // n_dp
    share = [lax.dynamic_slice_in_dim(codes_t, lanes[t] * width, width, 1) for t in range(n_dp)]
    tiles = {(0, 0): share[0]}
    for k in range(1, n_sh):
        tiles[0, k] = move(share[0], "shard", ring(n_sh, k))
    for t in range(1, n_dp):
        tiles[t, 0] = share[t]
        for k in range(1, n_sh):
            tiles[t, k] = move(tiles[0, k], "dp", ring(n_dp, t))

    q = queries_in[0]
    own = q.shape[0]
    q_held = {0: q}
    for k in relay(group):
        step = 1 if 2 * k <= group else group - 1
        pairs = [(s, s // group * group + (s + step) % group) for s in range(n_sh)]
        q_held[k] = move(q_held[(k - step) % group], "shard", pairs)
    q_pieces = [q_held[k] for k in range(group)]
    q_from = [(zp * group + lax.rem(zi - k + group, group)) * n_dp + x for k in range(group)]

    w_pieces, w_places = [], []
    for e in evens:
        for t in range(n_dp):
            pairs = []
            for d in range(n_dom):
                for c in range(n_dp):
                    pairs.append((d * n_dp + c, (d ^ e) * n_dp + (c + t) % n_dp))
            w_pieces.append(w_z if e == t == 0 else move(w_z, ("dom", "dp"), pairs))
    w_pieces += [move(piece, "dom", flip(n_dom, 1)) for piece in w_pieces]
    for core in range(2):
        for e in evens:
            for t in range(n_dp):
                for k in range(n_sh):
                    w_places.append(((dom ^ (e | core)) * n_sh + shards[k]) * n_dp + lanes[t])
    w_places = jnp.stack(w_places).astype(I32)
    if w_rows % 16:
        whole = jnp.concatenate(w_pieces).reshape(n_dev, w_rows, depth)
        order = jnp.zeros((n_dev,), I32).at[w_places].set(jnp.arange(n_dev, dtype=I32))
        w_pieces = [whole[order].reshape(1, n_dev * w_rows, depth)]
        w_offsets = jnp.zeros((1,), I32)
    else:
        w_offsets = w_places * w_rows

    held = subspaces // (n_sh * n_dp)
    owners = []
    for j in range(n_zp):
        for t in range(n_dp):
            owners.append((lax.rem(zp + j, n_zp) * group + zi) * n_dp + lax.rem(x + t, n_dp))
    blocks = jnp.stack(owners).astype(I32)

    order = [[(t, 0) for t in range(n_dp)]] + [[(t, k) for k in range(1, n_sh)] for t in range(n_dp)]
    bases = [shards[k] * pass_rows + lanes[t] * width for part in order for t, k in part]
    built = []
    for part in order:
        built.append(rebuild(place, blocks, held, sub, words, [tiles[key] for key in part], books))
    passages = [b[0] for b in built]
    tile_codes = [b[1] for b in built]

    def rows_of(array):
        return jnp.concatenate([lax.dynamic_slice_in_dim(array, f * own, own, 0) for f in q_from])[:, None]

    out_rows = depth // n_dev
    firsts = []
    for core in range(2):
        for e in evens:
            for owner in owners:
                firsts.append(((dom ^ (e | core)) * n_sh * n_dp + owner) * out_rows)
    frow = (jnp.stack(firsts).astype(I32)[:, None] + jnp.arange(out_rows, dtype=I32)[None, :]).reshape(-1, 1)

    own_part, other_part, *grads = main(
        w_offsets,
        jnp.stack(bases).astype(I32),
        blocks,
        held * (depth // subspaces),
        frow,
        rows_of(positive_ids[0]),
        rows_of(loss_weight[0].astype(F32)),
        q_pieces,
        w_pieces,
        passages,
    )

    summed = own_part + move(other_part, "dom", flip(n_dom, 1))
    summed = summed.reshape(len(evens), len(owners), out_rows, depth)
    weight_grad = summed[0, 0]
    book_grad = None
    for o in reversed(range(len(owners))):
        j, t = o // n_dp, o % n_dp
        part = word_grads(o, held, words, grads[o], tile_codes)
        if o:
            pairs = []
            for s in range(n_sh):
                for d in range(n_dp):
                    pairs.append((s * n_dp + d, (s + group * j) % n_sh * n_dp + (d + t) % n_dp))
            part = move(part, ("shard", "dp"), pairs)
        book_grad = part if book_grad is None else book_grad + part
    for i, e in enumerate(evens):
        for o in range(len(owners)):
            if i == o == 0:
                continue
            j, t = o // n_dp, o % n_dp
            pairs = []
            for d in range(n_dom):
                for s in range(n_sh):
                    for c in range(n_dp):
                        to = ((d ^ e) * n_sh + (s + group * j) % n_sh) * n_dp + (c + t) % n_dp
                        pairs.append(((d * n_sh + s) * n_dp + c, to))
            moved = move(summed[i, o], ("dom", "shard", "dp"), pairs)
            weight_grad = weight_grad + moved
    return (weight_grad, book_grad[None])


def solution(mesh):
    sizes = [mesh.shape[a] for a in ("dom", "shard", "dp")]
    return jax.shard_map(
        functools.partial(compute, *sizes),
        mesh=mesh,
        in_specs=(
            P("dom", ("shard", "dp"), None),
            P(("dom", "shard", "dp"), None),
            P("dom", "shard", None, None),
            P("dom", "shard", None),
            P("dom", None),
            P("dom", None),
        ),
        out_specs=(P(("dom", "shard", "dp"), None), P("dom", ("shard", "dp"), None, None)),
        check_vma=False,
    )
```
